32 devices in a mesh: col: 4 (over z), dp: 4 (over x, core), strip: 2 (over y).
Axes of the slice: x: 2, y: 2, z: 4, core: 2. Of those that a mesh axis runs over, the one named last changes fastest.
Arguments:
- stem: bfloat16 [16, 4, 32, 360], P('dp', 'strip'), may hold values from -6 to 6
- labels: int32 [16, 4, 32], P('dp', 'strip'), may hold values from 0 to 149
- up_proj: bfloat16 [4, 720, 360], P('col'), may hold values from -0.21875 to 0.21875
- mix_proj: bfloat16 [4, 360, 360], P('col'), may hold values from -0.3125 to 0.3125
- down_proj: bfloat16 [4, 360, 720], P('col'), may hold values from -0.3125 to 0.3125
- dw_kernel: bfloat16 [4, 9, 360], P('col'), may hold values from -2 to 2
- gain1: float32 [4, 360], P('col'), may hold values from 0.31622776 to 1
- gain2: float32 [4, 720], P('col'), may hold values from 0.31622776 to 1
- lat_one: bfloat16 [360, 512], replicated, may hold values from -0.3125 to 0.3125
- lat_two: bfloat16 [720, 512], replicated, may hold values from -0.21875 to 0.21875
- classifier: bfloat16 [512, 150], replicated, may hold values from -1.0546875 to 1.0546875
Outputs:
- grad_up: float32 [4, 720, 360], P('col', ('dp', 'strip'))
- grad_mix: float32 [4, 360, 360], P('col', ('dp', 'strip'))
- grad_down: float32 [4, 360, 720], P('col', ('dp', 'strip'))
- grad_kernel: float32 [4, 9, 360], P('col', None, ('dp', 'strip'))
- grad_stem: float32 [16, 4, 32, 360], P('dp', 'strip', 'col')
The draws below stay inside these ranges and needn't reach their ends.
All inputs are finite; a program needn't handle non-finite values.
Results may differ from the reference program's by a relative error of at most 0.034.
Values sent between devices are 32-bit elements; how exact they have to be, the bound alone decides.
A program may use at most 64 MiB of HBM per device.

```python
import math
import jax
import jax.numpy as jnp
from jax import lax

C1 = 360
C2 = 720
HEAD = 512
CLASSES = 150
W1 = 32
COLS = 4
BATCH = 16
H1 = 4


def plant(values, own_key, smallest, largest):
    longest = values.shape.index(max(values.shape))
    spots = []
    for shift in (0, 1):
        where = [jax.random.randint(jax.random.fold_in(own_key, axis), (), 0, length) for axis, length in enumerate(values.shape)]
        where[longest] = (where[longest] + shift) % values.shape[longest]
        spots.append(tuple(where))
    return values.at[spots[0]].set(smallest).at[spots[1]].set(largest)


def shard_levels(own_key, shape, cuts, low, top_value):
    def one(axis_at, parts):
        steps = jax.random.uniform(jax.random.fold_in(jax.random.fold_in(own_key, 6), axis_at), (parts,), jnp.float32, low / len(cuts), top_value / len(cuts))
        return jnp.repeat(jnp.exp(steps), shape[axis_at] // parts).reshape((-1,) + (1,) * (len(shape) - axis_at - 1))

    level = one(*cuts[0])
    for cut in cuts[1:]:
        level = level * one(*cut)
    return level


def noise(own_key, dims, scale, limit, cuts=(), kind=jnp.bfloat16):
    values = jax.random.normal(own_key, dims, jnp.float32) * scale
    if len(cuts) > 0:
        values = shard_levels(own_key, dims, cuts, -0.22, 0.18) * values
    return jnp.clip(values, min=-limit, max=limit).astype(kind)


def setup_inputs(seed: int = 0) -> dict:
    arg_keys = jax.random.split(jax.random.key(seed), 12)
    return {
        "stem": noise(arg_keys[0], (BATCH, H1, W1, C1), 1.0, 6.0, ((0, 4), (1, 2))),
        "labels": plant(jax.random.randint(arg_keys[1], (BATCH, H1, W1), 0, CLASSES), jax.random.fold_in(arg_keys[1], 1), 0, CLASSES - 1).astype(jnp.int32),
        "up_proj": noise(arg_keys[2], (COLS, C2, C1), C2 ** -0.5, 0.21875, ((0, 4),)),
        "mix_proj": noise(arg_keys[3], (COLS, C1, C1), C1 ** -0.5, 0.3125, ((0, 4),)),
        "down_proj": noise(arg_keys[4], (COLS, C1, C2), C1 ** -0.5, 0.3125, ((0, 4),)),
        "dw_kernel": noise(arg_keys[5], (COLS, 9, C1), 9 ** -0.5, 2.0, ((0, 4),)),
        "gain1": jnp.clip(jnp.exp(math.log(1.0) - 1.1512926 * jax.random.uniform(arg_keys[6], (COLS, C1), jnp.float32) ** shard_levels(arg_keys[6], (COLS, C1), ((0, 4),), -0.2, 0.2)), 0.31622776, 1.0),
        "gain2": jnp.clip(jnp.exp(math.log(1.0) - 1.1512926 * jax.random.uniform(arg_keys[7], (COLS, C2), jnp.float32) ** shard_levels(arg_keys[7], (COLS, C2), ((0, 4),), -0.2, 0.2)), 0.31622776, 1.0),
        "lat_one": noise(arg_keys[8], (C1, HEAD), C1 ** -0.5, 0.3125),
        "lat_two": noise(arg_keys[9], (C2, HEAD), C2 ** -0.5, 0.21875),
        "classifier": noise(arg_keys[10], (HEAD, CLASSES), (4.0 / HEAD ** 0.5), 1.0546875),
    }


loss_scale = 64.0
root_coef = 0.7978845608028654
cube_coef = 0.044715


def gelu_pair(values):
    inner = root_coef * (values + cube_coef * values * values * values)
    tangent = jnp.tanh(inner)
    result = 0.5 * values * (1.0 + tangent)
    slope = 0.5 * (1.0 + tangent) + 0.5 * values * (1.0 - tangent * tangent) * root_coef * (1.0 + 3.0 * cube_coef * values * values)
    return result, slope


def project(left, matrix):
    flat = left.reshape(-1, left.shape[-1])
    out = jnp.dot(flat, matrix, preferred_element_type=jnp.float32)
    return out.reshape(left.shape[:-1] + (matrix.shape[1],))


def project_back(left, matrix):
    flat = left.reshape(-1, left.shape[-1])
    out = lax.dot_general(flat, matrix, (((1,), (1,)), ((), ())), preferred_element_type=jnp.float32)
    return out.reshape(left.shape[:-1] + (matrix.shape[0],))


def outer_sum(left, right):
    return lax.dot_general(left.reshape(-1, left.shape[-1]), right.reshape(-1, right.shape[-1]), (((0,), (0,)), ((), ())), preferred_element_type=jnp.float32)


def upsample(values):
    return jnp.repeat(jnp.repeat(values, 2, axis=-3), 2, axis=-2)


def pool_sum(values):
    shape = values.shape
    return values.reshape(shape[:-3] + (shape[-3] // 2, 2, shape[-2] // 2, 2, shape[-1])).sum(axis=(-4, -2))


def depthwise_apply(padded, kernel):
    row_count = padded.shape[-3] - 2
    col_count = padded.shape[-2] - 2
    total = jnp.zeros(padded.shape[:-3] + (row_count, col_count, padded.shape[-1]), jnp.float32)
    for tap_index in range(9):
        row_shift = tap_index // 3 - 1
        col_shift = tap_index % 3 - 1
        total = total + kernel[tap_index] * padded[..., 1 + row_shift:1 + row_shift + row_count, 1 + col_shift:1 + col_shift + col_count, :]
    return total


def depthwise_adjoint(padded, kernel):
    row_count = padded.shape[-3] - 2
    col_count = padded.shape[-2] - 2
    total = jnp.zeros(padded.shape[:-3] + (row_count, col_count, padded.shape[-1]), jnp.float32)
    for tap_index in range(9):
        row_shift = tap_index // 3 - 1
        col_shift = tap_index % 3 - 1
        total = total + kernel[tap_index] * padded[..., 1 - row_shift:1 - row_shift + row_count, 1 - col_shift:1 - col_shift + col_count, :]
    return total


def kernel_terms(padded, grad_depth):
    row_count = grad_depth.shape[-3]
    col_count = grad_depth.shape[-2]
    axes = tuple(range(grad_depth.ndim - 1))
    pieces = []
    for tap_index in range(9):
        row_shift = tap_index // 3 - 1
        col_shift = tap_index % 3 - 1
        window = padded[..., 1 + row_shift:1 + row_shift + row_count, 1 + col_shift:1 + col_shift + col_count, :]
        pieces.append(jnp.sum(window * grad_depth, axis=axes))
    return jnp.stack(pieces, axis=0)


def head_grads(level_one, level_two, lat_one, lat_two, classifier, labels, npix):
    lateral = project(level_one.astype(jnp.bfloat16), lat_one) + upsample(project(level_two.astype(jnp.bfloat16), lat_two))
    active, slope = gelu_pair(lateral)
    hidden = active.astype(jnp.bfloat16)
    logits = project(hidden, classifier)
    probs = jax.nn.softmax(logits, axis=-1)
    onehot = (labels[..., None] == jnp.arange(classifier.shape[1], dtype=jnp.int32)).astype(jnp.float32)
    grad_logits = (probs - onehot) * (loss_scale / npix)
    grad_lat = project_back(grad_logits.astype(jnp.bfloat16), classifier) * slope
    cot_one = project_back(grad_lat.astype(jnp.bfloat16), lat_one)
    cot_two = project_back(pool_sum(grad_lat).astype(jnp.bfloat16), lat_two)
    return cot_one, cot_two


def pad_crop(values):
    return jnp.pad(values, ((0, 0), (1, 1), (1, 1), (0, 0)))


def reference(stem, labels, up_proj, mix_proj, down_proj, dw_kernel, gain1, gain2, lat_one, lat_two, classifier):
    columns = up_proj.shape[0]
    crops, height, width, chan_one = stem.shape
    chan_two = up_proj.shape[1]
    state_one = jnp.zeros((crops, height, width, chan_one), jnp.float32)
    state_two = jnp.zeros((crops, height // 2, width // 2, chan_two), jnp.float32)
    stem_wide = stem.astype(jnp.float32)
    saves = []
    for column in range(columns):
        kernel = dw_kernel[column].astype(jnp.float32)
        narrow = state_two.astype(jnp.bfloat16)
        mixture = stem_wide + upsample(project(narrow, up_proj[column]))
        padded = pad_crop(mixture)
        depth = depthwise_apply(padded, kernel)
        active, slope_one = gelu_pair(depth)
        hidden = active.astype(jnp.bfloat16)
        state_one = gain1[column] * state_one + project(hidden, mix_proj[column])
        pooled = (pool_sum(state_one) * 0.25).astype(jnp.bfloat16)
        lifted, slope_two = gelu_pair(project(pooled, down_proj[column]))
        state_two = gain2[column] * state_two + lifted
        saves.append((narrow, padded, slope_one, hidden, pooled, slope_two))
    npix = float(crops * height * width)
    cot_one, cot_two = head_grads(state_one, state_two, lat_one, lat_two, classifier, labels, npix)
    grads_up = [None] * columns
    grads_mix = [None] * columns
    grads_down = [None] * columns
    grads_kernel = [None] * columns
    grad_stem = jnp.zeros(stem.shape, jnp.float32)
    for column in range(columns - 1, -1, -1):
        narrow, padded, slope_one, hidden, pooled, slope_two = saves[column]
        kernel = dw_kernel[column].astype(jnp.float32)
        grad_lift = (cot_two * slope_two).astype(jnp.bfloat16)
        grads_down[column] = outer_sum(pooled, grad_lift)
        total_one = cot_one + upsample(project_back(grad_lift, down_proj[column])) * 0.25
        total_narrow = total_one.astype(jnp.bfloat16)
        grads_mix[column] = outer_sum(hidden, total_narrow)
        grad_depth = project_back(total_narrow, mix_proj[column]) * slope_one
        grads_kernel[column] = kernel_terms(padded, grad_depth)
        grad_mixture = depthwise_adjoint(pad_crop(grad_depth), kernel)
        grad_stem = grad_stem + grad_mixture
        grad_narrow = pool_sum(grad_mixture).astype(jnp.bfloat16)
        grads_up[column] = outer_sum(narrow, grad_narrow)
        cot_two = gain2[column] * cot_two + project_back(grad_narrow, up_proj[column])
        cot_one = gain1[column] * total_one
    return (jnp.stack(grads_up, 0), jnp.stack(grads_mix, 0), jnp.stack(grads_down, 0), jnp.stack(grads_kernel, 0), grad_stem)
```

```python
import contextlib
import functools

import jax
import jax.numpy as jnp
from jax import lax
from jax.experimental import pallas as pl
from jax.experimental.pallas import tpu as pltpu
from jax.sharding import PartitionSpec as P

loss_scale = 64.0
root_coef = 0.7978845608028654
cube_coef = 0.044715
f32 = jnp.float32
bf16 = jnp.bfloat16
MESH = pl.DeviceIdType.MESH
scope = contextlib.nullcontext


def gelu_pair(values):
    square = values * values
    tangent = jnp.tanh(root_coef * (values + cube_coef * values * square))
    half = 0.5 * (1.0 + tangent)
    slope = half + 0.5 * values * (1.0 - tangent * tangent) * root_coef * (
        1.0 + 3.0 * cube_coef * square
    )
    return values * half, slope


def dot(left, right):
    return jnp.dot(left, right, preferred_element_type=f32)


def dot_back(left, right):
    return lax.dot_general(left, right, (((1,), (1,)), ((), ())), preferred_element_type=f32)


def dot_outer(left, right):
    return lax.dot_general(left, right, (((0,), (0,)), ((), ())), preferred_element_type=f32)


def up_to(count, multiple):
    return -(-count // multiple) * multiple


def spread(count, owners, T):
    parts = owners * T
    run = count // parts
    half = up_to(run, 16) // 2
    source = lax.broadcasted_iota(jnp.int32, (count, 1), 0)
    target = source
    before = 0
    for owner in range(owners):
        for h in range(T):
            for side in range(2):
                begin = (owner * T + h) * run + side * half
                shift = ((owner * 2 + side) * T + h) * half - begin
                target = target + jnp.where(source >= begin, shift - before, 0)
                before = shift
    spot = lax.broadcasted_iota(jnp.int32, (count, parts * 2 * half), 1)
    return (spot == target).astype(f32).astype(bf16)


def pool_matrix(rows, width, axis_fine):
    fine, coarse = rows * width, rows * width // 4
    shape = (fine, coarse) if axis_fine == 0 else (coarse, fine)
    f = lax.broadcasted_iota(jnp.int32, shape, axis_fine)
    c = lax.broadcasted_iota(jnp.int32, shape, 1 - axis_fine)
    hit = jnp.zeros(shape, jnp.bool_)
    half = width // 2
    for row in range(rows // 2):
        rest = f - row * 2 * width
        inside = (rest >= 0) & (rest < 2 * width)
        rest = jnp.where(rest >= width, rest - width, rest)
        pos = 2 * (c - row * half)
        hit = hit | (inside & ((rest == pos) | (rest == pos + 1)))
    return hit.astype(f32).astype(bf16)


def kernel(
    S, D, T, M, rl, W, npix,
    stem, labels, up, mix, down, taps, gain1, gain2, lat1, lat2, cls,
    o_up, o_mix, o_down, o_taps, o_stem,
    stem_send, stem_full, lab_full, in1, in2, out1, out2, cin1, cin2, cout1, cout2,
    inp, outp, cinp, coutp, branch_s, hidden_c, pooled_c, narrow_c,
    pad, mixture_s, slope1_s, hidden_s, narrow_s, pooled_s, slope2_s, total_s, lift_s, gnar_s,
    spread_u, spread_p, gs_send, gs_recv, stem_sum, stem_far,
    acc_d, acc_m, acc_u, got_d, got_m, got_u, fx_d, fx_m, fx_u, fy_d, fy_m, fy_u,
    gx_d, gx_m, gx_u, gy_d, gy_m, gy_u, gk, gk_got, gk_pair, gk_x, gk_sum, gk_y,
    stem_ss, stem_rs, lab_ss, lab_rs, f_ss, f_rs, b_ss, b_rs, g_ss, g_rs, gy_ss, gy_rs,
    p_ss, p_rs, x1_ss, x1_rs, y1_ss, y1_rs, x2_ss, x2_rs, y2_ss, y2_rs,
    k_ss, k_rs, ff_ss, ff_rs, bb_ss, bb_rs,
):
    col, dp, strip = lax.axis_index("col"), lax.axis_index("dp"), lax.axis_index("strip")
    first, last = col == 0, col == S - 1
    C1, C2 = up.shape[1], up.shape[0]
    RW = rl * W
    pix = T * RW
    rows = T * rl
    wc = W // S
    par = lax.rem(dp, 2)
    mine = dp // 2
    Q = D // 2

    def remote(src, dst, ss, rs, target):
        return pltpu.make_async_remote_copy(
            src_ref=src, dst_ref=dst, send_sem=ss, recv_sem=rs,
            device_id=target, device_id_type=MESH,
        )

    gate = pltpu.get_barrier_semaphore()
    for h in range(T):
        for k in range(S):

            @pl.when((col != k) | (strip != h))
            def _():
                pl.semaphore_signal(
                    gate, inc=1, device_id={"col": k, "strip": h}, device_id_type=MESH
                )

        for d in range(D):

            @pl.when(dp != d)
            def _():
                pl.semaphore_signal(
                    gate, inc=1, device_id={"dp": d, "strip": h}, device_id_type=MESH
                )

    for m in range(M):
        for h in range(T):
            stem_send[h, m] = stem[h * M + m].astype(f32)

    @pl.when(first)
    def _():
        in1[...] = jnp.zeros_like(in1)
        in2[...] = jnp.zeros_like(in2)
        inp[...] = jnp.zeros_like(inp)

    @pl.when(last)
    def _():
        cinp[...] = jnp.zeros_like(cinp)

    pad[...] = jnp.zeros_like(pad)
    gk[...] = jnp.zeros_like(gk)
    spread_u[...] = pool_matrix(rows, W, 0)
    spread_p[...] = pool_matrix(rows, W, 1)
    with scope("gatewait"):
        pl.semaphore_wait(gate, S * T - 1 + (D - 1) * T)

    def stem_copy(h, m, slot):
        return remote(
            stem_send.at[h, m], stem_full.at[m, slot], stem_ss.at[h, m], stem_rs.at[slot, m],
            {"strip": h},
        )

    def lab_copy(h, m, slot):
        return remote(
            labels.at[h * M + m], lab_full.at[m, slot], lab_ss.at[h, m], lab_rs.at[slot, m],
            {"strip": h},
        )

    for m in range(M):
        for h in range(T):
            @pl.when(strip != h)
            def _():
                stem_copy(h, m, strip).start()
    for m in range(M):
        for h in range(T):

            @pl.when(strip != h)
            def _():
                lab_copy(h, m, strip).start()

            @pl.when(strip == h)
            def _():
                stem_full[m, h] = stem[h * M + m].astype(f32)
                lab_full[m, h] = labels[h * M + m]

    kern = taps[0:9].astype(f32)
    g1 = gain1[...]
    g2 = gain2[...]
    place = lax.rem(lax.broadcasted_iota(jnp.int32, (pix, 1), 0), W)
    not_low = place != 0
    not_high = place != W - 1

    def widen(values):
        return dot(spread_u[...], values).astype(bf16)

    def pool(values):
        high = values.astype(bf16)
        low = (values - high.astype(f32)).astype(bf16)
        return dot(spread_p[...], high) + dot(spread_p[...], low)

    def sides(values):
        pad[8 : 8 + pix] = values
        before = jnp.where(not_low, pad[7 : 7 + pix], 0.0)
        after = jnp.where(not_high, pad[9 : 9 + pix], 0.0)
        return before, values, after

    def rows_moved(values, step):
        if step == 0:
            return values
        blank = jnp.zeros((W, values.shape[1]), f32)
        if step > 0:
            return jnp.concatenate([values[W:], blank], axis=0)
        return jnp.concatenate([blank, values[:-W]], axis=0)

    def depthwise(values, sign):
        trio = sides(values)
        total = None
        for i in (-1, 0, 1):
            line = None
            for j in (-1, 0, 1):
                t = 3 * (i + 1) + (j + 1)
                term = kern[t : t + 1] * trio[1 + sign * j]
                line = term if line is None else line + term
            line = rows_moved(line, sign * i)
            total = line if total is None else total + line
        return total

    def f_copy(n, m):
        src, dst = (None, (out2, in2), (outp, inp))[n]
        return remote(src.at[m], dst.at[m], f_ss.at[n, m], f_rs.at[n, m], {"col": col + 1})

    def b_copy(n, m):
        src, dst = (None, (cout2, cin2), (coutp, cinp))[n]
        return remote(src.at[m], dst.at[m], b_ss.at[n, m], b_rs.at[n, m], {"col": col - 1})

    def f_row(m, r):
        part = pl.ds(r * W, W)
        return remote(
            out1.at[m, part], in1.at[m, part], ff_ss.at[m, r], ff_rs.at[m, r], {"col": col + 1}
        )

    def b_row(m, r):
        part = pl.ds(r * W, W)
        return remote(
            cout1.at[m, part], cin1.at[m, part], bb_ss.at[m, r], bb_rs.at[m, r],
            {"col": col - 1},
        )

    def forward(m, carry):
        with scope("f_stemwait"):
            for h in range(T):

                @pl.when(strip != h)
                def _():
                    stem_copy(h, m, h).wait_recv()

        with scope("f_wait1"):
            @pl.when(jnp.logical_not(first))
            def _():
                f_copy(1, m).wait_recv()

        narrow = in2[m].astype(bf16)
        narrow_s[m] = narrow
        mixture = stem_full[m].reshape(pix, C1) + dot(widen(narrow), up[...])
        mixture_s[m] = mixture
        active, slope = gelu_pair(depthwise(mixture, 1))
        slope1_s[m] = slope
        hidden = active.astype(bf16)
        hidden_s[m] = hidden
        branch = dot(hidden, mix[...])
        branch_s[m] = branch
        pool_branch = pool(branch)

        with scope("f_wait2"):
            @pl.when(jnp.logical_not(first))
            def _():
                f_copy(2, m).wait_recv()

        low1 = g1 * inp[m] + pool_branch
        outp[m] = low1
        pooled = (low1 * 0.25).astype(bf16)
        pooled_s[m] = pooled
        lifted, slope2 = gelu_pair(dot(pooled, down[...]))
        slope2_s[m] = slope2
        out2[m] = g2 * in2[m] + lifted

        @pl.when(jnp.logical_not(last))
        def _():
            f_copy(1, m).start()
            f_copy(2, m).start()

        return carry

    with scope("FWD"):
        lax.fori_loop(0, M, forward, 0)

    def full_state(m):
        for r in range(rows):

            @pl.when(jnp.logical_not(first))
            def _():
                f_row(m, r).wait_recv()

            part = pl.ds(r * W, W)
            out1[m, part] = g1 * in1[m, part] + branch_s[m, part]

            @pl.when(jnp.logical_not(last))
            def _():
                f_row(m, r).start()

    def g_copy(k, m, sk):
        return remote(
            gs_send.at[k, m], gs_recv.at[sk, m], g_ss.at[k, m], g_rs.at[sk, m], {"col": k}
        )

    def stem_out(m, low, high):
        for k in range(S):

            @pl.when((col != k) & (k >= col + low) & (k < col + high))
            def _():
                g_copy(k, m, col).start()

    n = D * T
    flat = lambda ref: ref[...].reshape(-1, ref.shape[-1])
    accs, gots = (acc_d, acc_m, acc_u), (got_d, got_m, got_u)
    fxs, fys = (fx_d, fx_m, fx_u), (fy_d, fy_m, fy_u)
    gxs, gys = (gx_d, gx_m, gx_u), (gy_d, gy_m, gy_u)

    def chunked():
        pick = spread(C1, D, T)
        hidden_c[...] = dot(flat(hidden_s), pick).astype(bf16)
        pooled_c[...] = dot(flat(pooled_s), pick).astype(bf16)
        narrow_c[...] = dot(flat(narrow_s), spread(C2, D, T)).astype(bf16)

    partner = {"dp": dp + 1 - 2 * par}

    def p_copy(i, q):
        return remote(
            accs[i].at[q, 1 - par], gots[i].at[q], p_ss.at[i, q], p_rs.at[i, q], partner
        )

    def x1_copy(i, q, sq):
        return remote(
            accs[i].at[q, par, 0], fxs[i].at[sq], x1_ss.at[i, q], x1_rs.at[i, sq],
            {"dp": 2 * q + par},
        )

    def y1_copy(i, q, h, sh):
        return remote(
            accs[i].at[q, par, 1, h], fys[i].at[sh, q], y1_ss.at[i, h, q], y1_rs.at[i, sh, q],
            {"strip": h},
        )

    def x2_copy(i, q, sq):
        return remote(
            accs[i].at[q, par, 1, strip], gxs[i].at[sq], x2_ss.at[i, q], x2_rs.at[i, sq],
            {"dp": 2 * q + par},
        )

    def y2_copy(i, h, sh):
        return remote(
            accs[i].at[mine, par, 0, h], gys[i].at[sh], y2_ss.at[i, h], y2_rs.at[i, sh],
            {"strip": h},
        )

    def store_grad(i, left, right):
        accs[i][...] = dot_outer(left[...], flat(right)).reshape(accs[i].shape)
        for q in range(Q):
            p_copy(i, q).start()

    def down_grad():
        store_grad(0, pooled_c, lift_s)

    def backward(m, carry):
        @pl.when(last)
        def _():
            with scope("h_state"):
                full_state(m)
                for h in range(T):

                    @pl.when(strip != h)
                    def _():
                        lab_copy(h, m, h).wait_recv()

            lateral = dot(out1[m].astype(bf16), lat1[...]) + dot(
                widen(out2[m].astype(bf16)), lat2[...]
            )
            active, slope = gelu_pair(lateral)
            logits = dot_back(active.astype(bf16), cls[...])
            shifted = jnp.exp(logits - jnp.max(logits, axis=-1, keepdims=True))
            probs = shifted / jnp.sum(shifted, axis=-1, keepdims=True)
            eye = lax.broadcasted_iota(jnp.int32, (W, W), 0) == lax.broadcasted_iota(
                jnp.int32, (W, W), 1
            )
            lines = []
            for h in range(T):
                block = lab_full[m, h].astype(f32)
                for r in range(rl):
                    turned = jnp.where(eye, block[r : r + 1], 0.0)
                    lines.append(jnp.sum(turned, axis=1, keepdims=True))
            label = jnp.concatenate(lines, axis=0).astype(jnp.int32)
            onehot = (lax.broadcasted_iota(jnp.int32, logits.shape, 1) == label).astype(f32)
            grad_logits = (probs - onehot) * (loss_scale / npix)
            grad_lat = dot(grad_logits.astype(bf16), cls[...]) * slope
            cin1[m] = dot_back(grad_lat.astype(bf16), lat1[...])
            cin2[m] = dot_back(pool(grad_lat).astype(bf16), lat2[...])

        for r in range(rows):

            @pl.when(jnp.logical_not(last))
            def _():
                b_row(m, r).wait_recv()

            @pl.when(jnp.logical_not(first))
            def _():
                part = pl.ds(r * W, W)
                cout1[m, part] = g1 * cin1[m, part]
                b_row(m, r).start()

        with scope("b_wait1"):
            @pl.when(jnp.logical_not(last))
            def _():
                b_copy(1, m).wait_recv()

        cot2 = cin2[m]
        lift = (cot2 * slope2_s[m]).astype(bf16)
        lift_s[m] = lift
        rise = dot_back(lift, down[...]) * 0.25

        @pl.when(first & (m == M - 1))
        def _():
            down_grad()

        @pl.when(jnp.logical_not(last))
        def _():
            b_copy(2, m).wait_recv()

        rise = cinp[m] + rise

        @pl.when(jnp.logical_not(first))
        def _():
            coutp[m] = g1 * rise
            b_copy(2, m).start()

        high = rise.astype(bf16)
        low = (rise - high.astype(f32)).astype(bf16)
        total = cin1[m] + (dot(spread_u[...], high) + dot(spread_u[...], low))
        total_narrow = total.astype(bf16)
        total_s[m] = total_narrow
        grad_depth = dot_back(total_narrow, mix[...]) * slope1_s[m]
        grad_mixture = depthwise(grad_depth, -1)
        grad_narrow = pool(grad_mixture).astype(bf16)
        gnar_s[m] = grad_narrow
        cout2[m] = g2 * cot2 + dot_back(grad_narrow, up[...])

        with scope("b_send1"):
            @pl.when(jnp.logical_not(first))
            def _():
                b_copy(1, m).start()

        cube = grad_mixture.reshape(rows, W, C1)
        for k in range(S):
            for h in range(T):
                gs_send[k, m, h] = cube[h * rl : (h + 1) * rl, k * wc : (k + 1) * wc]
        for k in range(S):

            @pl.when(col == k)
            def _():
                gs_recv[k, m] = gs_send[k, m]

        @pl.when(first)
        def _():
            stem_out(m, 1, S)

        trio = sides(mixture_s[m])
        for i in (-1, 0, 1):
            for j in (-1, 0, 1):
                t = 3 * (i + 1) + (j + 1)
                window = rows_moved(trio[1 + j], i)
                gk[t : t + 1] += jnp.sum(window * grad_depth, axis=0, keepdims=True)
        return carry

    @pl.when(jnp.logical_not(last))
    def _():
        for m in range(M):
            full_state(m)
        chunked()

    with scope("BWD"):
        lax.fori_loop(0, M, backward, 0)

    @pl.when(last)
    def _():
        chunked()

    @pl.when(jnp.logical_not(first))
    def _():
        for m in range(M):
            stem_out(m, 1, S)

    def k_copy(stage, src, dst, target, t, st):
        return remote(src, dst, k_ss.at[stage, t], k_rs.at[stage, st], target)

    def kp():
        return k_copy(0, gk, gk_got, partner, 0, 0)

    def kx(q, sq):
        return k_copy(1, gk_pair, gk_x.at[sq], {"dp": 2 * q + par}, q, sq)

    def ky(h, sh):
        return k_copy(2, gk_sum, gk_y.at[sh], {"strip": h}, h, sh)

    def others(count, me, act):
        for t in range(count):

            @pl.when(me != t)
            def _():
                act(t)

    kp().start()

    @pl.when(jnp.logical_not(first))
    def _():
        down_grad()

    with scope("w_mm"):
        store_grad(1, hidden_c, total_s)
        store_grad(2, narrow_c, gnar_s)
    kp().wait_recv()
    gk_pair[...] = gk[...] + gk_got[...]
    others(Q, mine, lambda q: kx(q, mine).start())
    for i in range(3):
        with scope("w_pair"):
            for q in range(Q):
                p_copy(i, q).wait_recv()
                accs[i][q, par] += gots[i][q]
            others(Q, mine, lambda q: x1_copy(i, q, mine).start())

        def send_y(h):
            for q in range(Q):
                y1_copy(i, q, h, strip).start()

        others(T, strip, send_y)

    @pl.when(jnp.logical_not(first))
    def _():
        for m in range(M):
            stem_out(m, -1, 0)

    gk_sum[...] = gk_pair[...]

    def add_kx(q):
        kx(q, q).wait_recv()
        gk_sum[...] += gk_x[q]

    others(Q, mine, add_kx)
    others(T, strip, lambda h: ky(h, strip).start())

    def gy_copy(h, sh):
        return remote(
            stem_sum.at[h], stem_far.at[sh], gy_ss.at[h], gy_rs.at[sh], {"strip": h}
        )

    def stem_total():
        def landed(k):
            for m in range(M):
                g_copy(k, m, k).wait_recv()

        others(S, col, landed)
        for h in range(T):
            for m in range(M):
                total = gs_recv[0, m, h]
                for k in range(1, S):
                    total = total + gs_recv[k, m, h]
                stem_sum[h, m] = total
        others(T, strip, lambda h: gy_copy(h, strip).start())

    with scope("w_stem1"):
        pl.when(first)(stem_total)

    for i in range(3):

        def add_x(q):
            x1_copy(i, q, q).wait_recv()
            accs[i][mine, par, 0] += fxs[i][q]

        with scope("w_addx"):
            others(Q, mine, add_x)
            others(T, strip, lambda h: y2_copy(i, h, strip).start())

        def add_y(h):
            for q in range(Q):
                y1_copy(i, q, h, h).wait_recv()
                accs[i][q, par, 1, strip] += fys[i][h, q]

        with scope("w_addy"):
            others(T, strip, add_y)
            others(Q, mine, lambda q: x2_copy(i, q, mine).start())

    @pl.when(jnp.logical_not(first))
    def _():
        with scope("w_stem2"):
            for m in range(M):
                stem_out(m, -S, -1)
            stem_total()

    def add_ky(h):
        ky(h, h).wait_recv()

    others(T, strip, add_ky)
    share_k = gk_sum[...]
    for h in range(T):
        share_k = share_k + jnp.where(strip != h, gk_y[h], 0.0)
    w = C1 // n
    share = share_k[0:9, 0:w]
    for k in range(1, n):
        share = jnp.where(dp * T + strip == k, share_k[0:9, k * w : (k + 1) * w], share)
    o_taps[...] = share

    for i, out in enumerate((o_down, o_mix, o_up)):

        def last_y(h):
            y2_copy(i, h, h).wait_recv()
            accs[i][mine, par, 0, strip] += gys[i][h]

        with scope("w_lasty"):
            others(T, strip, last_y)

        def last_x(q):
            x2_copy(i, q, q).wait_recv()
            accs[i][mine, par, 1, strip] += gxs[i][q]

        with scope("w_lastx"):
            others(Q, mine, last_x)
        half = accs[i].shape[4]
        out[0:half] = accs[i][mine, par, 0, strip]
        out[half:] = accs[i][mine, par, 1, strip][0 : out.shape[0] - half]

    for h in range(T):
        rows_h = slice(h * M, (h + 1) * M)

        @pl.when(strip == h)
        def _():
            o_stem[rows_h] = stem_sum[h]

        @pl.when(strip != h)
        def _():
            gy_copy(h, h).wait_recv()
            o_stem[rows_h] = stem_far[h]

    for m in range(M):
        for h in range(T):

            @pl.when(strip != h)
            def _():
                stem_copy(h, m, strip).wait_send()
                lab_copy(h, m, strip).wait_send()

                @pl.when(jnp.logical_not(last))
                def _():
                    lab_copy(h, m, h).wait_recv()

        @pl.when(jnp.logical_not(last))
        def _():
            f_copy(1, m).wait_send()
            f_copy(2, m).wait_send()
            for r in range(rows):
                f_row(m, r).wait_send()

        @pl.when(jnp.logical_not(first))
        def _():
            b_copy(1, m).wait_send()
            b_copy(2, m).wait_send()
            for r in range(rows):
                b_row(m, r).wait_send()

    def sent_stem(k):
        for m in range(M):
            g_copy(k, m, col).wait_send()

    others(S, col, sent_stem)
    others(T, strip, lambda h: gy_copy(h, strip).wait_send())
    kp().wait_send()
    others(Q, mine, lambda q: kx(q, mine).wait_send())
    others(T, strip, lambda h: ky(h, strip).wait_send())
    for i in range(3):
        for q in range(Q):
            p_copy(i, q).wait_send()

        def sent_x(q):
            x1_copy(i, q, mine).wait_send()
            x2_copy(i, q, mine).wait_send()

        def sent_y(h):
            for q in range(Q):
                y1_copy(i, q, h, strip).wait_send()
            y2_copy(i, h, strip).wait_send()

        others(Q, mine, sent_x)
        others(T, strip, sent_y)


def finish(*refs):
    for source, target in zip(refs[:4], refs[5:9]):
        target[...] = source[...].reshape(target.shape)
    refs[9][...] = refs[4][...]


def shards(stem, labels, up, mix, down, taps, gain1, gain2, lat1, lat2, cls):
    B, rl, W, C1 = stem.shape
    C2 = up.shape[1]
    S, D, T = lax.axis_size("col"), lax.axis_size("dp"), lax.axis_size("strip")
    M = B // T
    RW = rl * W
    pix = T * RW
    small = pix // 4
    wc = W // S
    n = D * T
    Q = D // 2
    p1, p2 = up_to(C1 // n, 16), up_to(C2 // n, 16)
    halves = ((p1 // 2, C2), (p1 // 2, C1), (p2 // 2, C1))
    npix = float(B * D * rl * T * W)
    V = pltpu.VMEM
    dma = pltpu.SemaphoreType.DMA
    vspec = pl.BlockSpec(memory_space=pltpu.VMEM)
    outs = pl.pallas_call(
        functools.partial(kernel, S, D, T, M, rl, W, npix),
        out_shape=(
            jax.ShapeDtypeStruct((C2 // n, C1), f32),
            jax.ShapeDtypeStruct((C1 // n, C1), f32),
            jax.ShapeDtypeStruct((C1 // n, C2), f32),
            jax.ShapeDtypeStruct((9, C1 // n), f32),
            jax.ShapeDtypeStruct((B, rl, wc, C1), f32),
        ),
        in_specs=[vspec] * 11,
        out_specs=(vspec,) * 5,
        scratch_shapes=[
            V((T, M, RW, C1), f32),
            V((M, T, RW, C1), f32),
            V((M, T, rl, W), jnp.int32),
            V((M, pix, C1), f32),
            V((M, small, C2), f32),
            V((M, pix, C1), f32),
            V((M, small, C2), f32),
            V((M, pix, C1), f32),
            V((M, small, C2), f32),
            V((M, pix, C1), f32),
            V((M, small, C2), f32),
            V((M, small, C1), f32),
            V((M, small, C1), f32),
            V((M, small, C1), f32),
            V((M, small, C1), f32),
            V((M, pix, C1), f32),
            V((M * pix, n * p1), bf16),
            V((M * small, n * p1), bf16),
            V((M * small, n * p2), bf16),
            V((pix + 16, C1), f32),
            V((M, pix, C1), f32),
            V((M, pix, C1), f32),
            V((M, pix, C1), bf16),
            V((M, small, C2), bf16),
            V((M, small, C1), bf16),
            V((M, small, C2), f32),
            V((M, pix, C1), bf16),
            V((M, small, C2), bf16),
            V((M, small, C1), bf16),
            V((pix, small), bf16),
            V((small, pix), bf16),
            V((S, M, T, rl, wc, C1), f32),
            V((S, M, T, rl, wc, C1), f32),
            V((T, M, rl, wc, C1), f32),
            V((T, M, rl, wc, C1), f32),
            *[V((Q, 2, 2, T, h, c), f32) for h, c in halves],
            *[V((Q, 2, T, h, c), f32) for h, c in halves],
            *[V((Q, T, h, c), f32) for h, c in halves],
            *[V((T, Q, h, c), f32) for h, c in halves],
            *[V((Q, h, c), f32) for h, c in halves],
            *[V((T, h, c), f32) for h, c in halves],
            V((16, C1), f32),
            V((16, C1), f32),
            V((16, C1), f32),
            V((Q, 16, C1), f32),
            V((16, C1), f32),
            V((T, 16, C1), f32),
            dma((T, M)),
            dma((T, M)),
            dma((T, M)),
            dma((T, M)),
            dma((3, M)),
            dma((3, M)),
            dma((3, M)),
            dma((3, M)),
            dma((S, M)),
            dma((S, M)),
            dma((T,)),
            dma((T,)),
            dma((3, Q)),
            dma((3, Q)),
            dma((3, Q)),
            dma((3, Q)),
            dma((3, T, Q)),
            dma((3, T, Q)),
            dma((3, Q)),
            dma((3, Q)),
            dma((3, T)),
            dma((3, T)),
            dma((3, max(Q, T))),
            dma((3, max(Q, T))),
            dma((M, T * rl)),
            dma((M, T * rl)),
            dma((M, T * rl)),
            dma((M, T * rl)),
        ],
        compiler_params=pltpu.CompilerParams(
            collective_id=0, has_side_effects=True, vmem_limit_bytes=60000 * 1024
        ),
        name="columns",
    )(
        stem.reshape(B, RW, C1), labels, up[0], mix[0], down[0], taps[0], gain1, gain2,
        lat1, lat2, cls.T,
    )
    tall = lambda a: jax.ShapeDtypeStruct((a.shape[0], 1, a.shape[1]), f32)
    done = pl.pallas_call(
        finish,
        out_shape=tuple(tall(a) for a in outs[:4])
        + (jax.ShapeDtypeStruct(outs[4].shape, f32),),
        in_specs=[vspec] * 5,
        out_specs=(vspec,) * 5,
        name="finish",
    )(*outs)
    return tuple(jnp.transpose(a, (1, 0, 2)) for a in done[:4]) + (done[4],)


def solution(mesh):
    placed = (
        P("dp", "strip", None, None),
        P("dp", "strip", None),
        P("col", None, None),
        P("col", None, None),
        P("col", None, None),
        P("col", None, None),
        P("col", None),
        P("col", None),
        P(),
        P(),
        P(),
    )
    return jax.shard_map(
        shards,
        mesh=mesh,
        in_specs=placed,
        out_specs=(
            P("col", ("dp", "strip"), None),
            P("col", ("dp", "strip"), None),
            P("col", ("dp", "strip"), None),
            P("col", None, ("dp", "strip")),
            P("dp", "strip", "col", None),
        ),
        check_vma=False,
    )
```

```python
import contextlib
import functools

import jax
import jax.numpy as jnp
from jax import lax
from jax.experimental import pallas as pl
from jax.experimental.pallas import tpu as pltpu
from jax.sharding import PartitionSpec as P

loss_scale = 64.0
root_coef = 0.7978845608028654
cube_coef = 0.044715
f32 = jnp.float32
bf16 = jnp.bfloat16
MESH = pl.DeviceIdType.MESH
scope = contextlib.nullcontext


def gelu_pair(values):
    square = values * values
    tangent = jnp.tanh(root_coef * (values + cube_coef * values * square))
    half = 0.5 * (1.0 + tangent)
    slope = half + 0.5 * values * (1.0 - tangent * tangent) * root_coef * (
        1.0 + 3.0 * cube_coef * square
    )
    return values * half, slope


def dot(left, right):
    return jnp.dot(left, right, preferred_element_type=f32)


def dot_back(left, right):
    return lax.dot_general(left, right, (((1,), (1,)), ((), ())), preferred_element_type=f32)


def dot_outer(left, right):
    return lax.dot_general(left, right, (((0,), (0,)), ((), ())), preferred_element_type=f32)


def up_to(count, multiple):
    return -(-count // multiple) * multiple


def spread(count, owners, T):
    parts = owners * T
    run = count // parts
    half = up_to(run, 16) // 2
    source = lax.broadcasted_iota(jnp.int32, (count, 1), 0)
    target = source
    before = 0
    for owner in range(owners):
        for h in range(T):
            for side in range(2):
                begin = (owner * T + h) * run + side * half
                shift = ((owner * 2 + side) * T + h) * half - begin
                target = target + jnp.where(source >= begin, shift - before, 0)
                before = shift
    spot = lax.broadcasted_iota(jnp.int32, (count, parts * 2 * half), 1)
    return (spot == target).astype(f32).astype(bf16)


def phase_matrix(rl, W):
    count, wide, quarter = rl * W, W // 2, rl * W // 4
    out = lax.broadcasted_iota(jnp.int32, (count, count), 0)
    source = lax.broadcasted_iota(jnp.int32, (count, count), 1)
    hit = jnp.zeros((count, count), jnp.bool_)
    for ri in range(2):
        for ci in range(2):
            for row in range(rl // 2):
                rest = out - ((2 * ri + ci) * quarter + row * wide)
                inside = (rest >= 0) & (rest < wide)
                hit = hit | (inside & (source == (2 * row + ri) * W + ci + 2 * rest))
    return hit.astype(f32).astype(bf16)


def kernel(
    S, D, T, M, rl, W, npix, cuts,
    stem_h, up_h, mix_h, down_h, lat1_h, lat2_h, cls, labels, taps, gain1, gain2,
    o_up, o_mix, o_down, o_taps, o_stem,
    stem, up, mix, down, lat1, lat2,
    stem_send, stem_full, lab_full, in1, in2, out1, out2, cin1, cin2, cout1, cout2,
    inp, outp, cinp, coutp, branch_s, hidden_c, pooled_c, narrow_c,
    mixture_s, slope1_s, hidden_s, narrow_s, pooled_s, slope2_s, total_s, lift_s, gnar_s,
    natural, gs_send, gs_recv, stem_sum, stem_far,
    acc_d, acc_m, acc_u, got_d, got_m, got_u, fx_d, fx_m, fx_u, fy_d, fy_m, fy_u,
    gx_d, gx_m, gx_u, gy_d, gy_m, gy_u, gk, gk_got, gk_pair, gk_x, gk_sum, gk_y,
    load_s,
    stem_ss, stem_rs, lab_ss, lab_rs, f_ss, f_rs, b_ss, b_rs, g_ss, g_rs, gy_ss, gy_rs,
    p_ss, p_rs, x1_ss, x1_rs, y1_ss, y1_rs, x2_ss, x2_rs, y2_ss, y2_rs,
    k_ss, k_rs, ff_ss, ff_rs, bb_ss, bb_rs,
):
    col, dp, strip = lax.axis_index("col"), lax.axis_index("dp"), lax.axis_index("strip")
    first, last = col == 0, col == S - 1
    C1, C2 = up.shape[1], up.shape[0]
    pix = T * rl * W
    small = pix // 4
    rows = T * rl
    wide = W // 2
    wc = W // S
    NC = len(cuts)
    lanes = [(a, min(a + 128, C1)) for a in range(0, C1, 128)]
    par = lax.rem(dp, 2)
    mine = dp // 2
    Q = D // 2

    def remote(src, dst, ss, rs, target):
        return pltpu.make_async_remote_copy(
            src_ref=src, dst_ref=dst, send_sem=ss, recv_sem=rs,
            device_id=target, device_id_type=MESH,
        )

    gate = pltpu.get_barrier_semaphore()
    for h in range(T):
        for k in range(S):

            @pl.when((col != k) | (strip != h))
            def _():
                pl.semaphore_signal(
                    gate, inc=1, device_id={"col": k, "strip": h}, device_id_type=MESH
                )

        for d in range(D):

            @pl.when(dp != d)
            def _():
                pl.semaphore_signal(
                    gate, inc=1, device_id={"dp": d, "strip": h}, device_id_type=MESH
                )

    loads = [
        pltpu.make_async_copy(src, dst, load_s.at[i])
        for i, (src, dst) in enumerate(
            ((stem_h, stem), (up_h, up), (mix_h, mix), (down_h, down),
             (lat1_h, lat1), (lat2_h, lat2))
        )
    ]
    for load in loads[:4]:
        load.start()

    @pl.when(last)
    def _():
        for load in loads[4:]:
            load.start()

    @pl.when(first)
    def _():
        in2[...] = jnp.zeros_like(in2)
        in1[...] = jnp.zeros_like(in1)
        inp[...] = jnp.zeros_like(inp)

    gk[...] = jnp.zeros_like(gk)
    order = phase_matrix(rl, W)
    loads[0].wait()
    for m in range(M):
        for h in range(T):
            stem_send[h, m] = dot(order, stem[h * M + m]).reshape(stem_send.shape[2:])
    with scope("gatewait"):
        pl.semaphore_wait(gate, S * T - 1 + (D - 1) * T)

    def stem_copy(h, m, slot):
        return remote(
            stem_send.at[h, m], stem_full.at[m, :, slot], stem_ss.at[h, m], stem_rs.at[slot, m],
            {"strip": h},
        )

    def lab_copy(h, m, slot):
        return remote(
            labels.at[h * M + m], lab_full.at[m, slot], lab_ss.at[h, m], lab_rs.at[slot, m],
            {"strip": h},
        )

    for m in range(M):
        for h in range(T):

            @pl.when(strip != h)
            def _():
                stem_copy(h, m, strip).start()

    for m in range(M):
        for h in range(T):

            @pl.when(strip != h)
            def _():
                lab_copy(h, m, strip).start()

            @pl.when(strip == h)
            def _():
                stem_full[m, :, h] = stem_send[h, m]
                lab_full[m, h] = labels[h * M + m]

    for load in loads[1:4]:
        load.wait()
    kern = taps[0:9].astype(f32)
    g1 = gain1[...]
    g2 = gain2[...]
    place = lax.rem(lax.broadcasted_iota(jnp.int32, (small, 1), 0), wide)
    not_low = place != 0
    not_high = place != wide - 1

    def split(values):
        return [[values[(2 * ri + ci) * small :][:small] for ci in range(2)] for ri in range(2)]

    def join(parts):
        return jnp.concatenate([parts[ri][ci] for ri in range(2) for ci in range(2)], axis=0)

    def pool(values):
        return (values[0:small] + values[small : 2 * small]) + (
            values[2 * small : 3 * small] + values[3 * small :]
        )

    def sources(parts):
        found = []
        for ri in range(2):
            even, odd = parts[ri]
            before = jnp.where(not_low, pltpu.roll(odd, 1, 0), 0.0)
            after = jnp.where(not_high, pltpu.roll(even, small - 1, 0), 0.0)
            found.append(((before, even, odd), (even, odd, after)))
        return found

    def rows_moved(values, step):
        if step == 0:
            return values
        blank = jnp.zeros((wide, values.shape[1]), f32)
        if step > 0:
            return jnp.concatenate([values[wide:], blank], axis=0)
        return jnp.concatenate([blank, values[:-wide]], axis=0)

    def depthwise(values, sign):
        found = sources(split(values))
        parts = [[None, None], [None, None]]
        for ri in range(2):
            for ci in range(2):
                total = None
                for i in (-1, 0, 1):
                    line = None
                    for j in (-1, 0, 1):
                        t = 3 * (sign * i + 1) + (sign * j + 1)
                        term = kern[t : t + 1] * found[(ri + i) % 2][ci][j + 1]
                        line = term if line is None else line + term
                    line = rows_moved(line, (ri + i) // 2)
                    total = line if total is None else total + line
                parts[ri][ci] = total
        return join(parts)

    def tap_sums(values, grads):
        found, grads = sources(split(values)), split(grads)
        lines = []
        for i in (-1, 0, 1):
            for j in (-1, 0, 1):
                total = None
                for ri in range(2):
                    for ci in range(2):
                        window, grad = found[(ri + i) % 2][ci][j + 1], grads[ri][ci]
                        step = (ri + i) // 2
                        if step > 0:
                            window, grad = window[wide:], grad[:-wide]
                        elif step < 0:
                            window, grad = window[:-wide], grad[wide:]
                        both = window * grad
                        for at in range(0, both.shape[0], wide):
                            piece = both[at : at + wide]
                            total = piece if total is None else total + piece
                lines.append(jnp.sum(total, axis=0, keepdims=True))
        return lines

    def f_copy(m, k):
        src, dst = (out2.at[m, k], in2.at[m, k]) if k < NC else (outp.at[m], inp.at[m])
        return remote(src, dst, f_ss.at[m, k], f_rs.at[m, k], {"col": col + 1})

    def b_copy(m, k):
        src, dst = (cout2.at[m, k], cin2.at[m, k]) if k < NC else (coutp.at[m], cinp.at[m])
        return remote(src, dst, b_ss.at[m, k], b_rs.at[m, k], {"col": col - 1})

    def f_row(m, r):
        return remote(
            out1.at[m, r], in1.at[m, r], ff_ss.at[m, r], ff_rs.at[m, r], {"col": col + 1}
        )

    def b_row(m, r):
        return remote(
            cout1.at[m, r], cin1.at[m, r], bb_ss.at[m, r], bb_rs.at[m, r], {"col": col - 1}
        )

    def forward(m, carry):
        with scope("f_stemwait"):
            for h in range(T):

                @pl.when(strip != h)
                def _():
                    stem_copy(h, m, h).wait_recv()

        risen = None
        for k, (a, b) in enumerate(cuts):
            with scope("f_wait1"):

                @pl.when(jnp.logical_not(first))
                def _():
                    f_copy(m, k).wait_recv()

            narrow = in2[m, k, :, 0 : b - a].astype(bf16)
            narrow_s[m, :, a:b] = narrow
            part = dot(narrow, up[a:b])
            risen = part if risen is None else risen + part
        mixture = stem_full[m].reshape(pix, C1) + jnp.concatenate([risen] * 4, axis=0)
        mixture_s[m] = mixture
        active, slope = gelu_pair(depthwise(mixture, 1))
        slope1_s[m] = slope
        hidden = active.astype(bf16)
        hidden_s[m] = hidden
        branch = dot(hidden, mix[...])
        branch_s[m] = branch[small:].reshape(branch_s.shape[1:])
        pool_branch = pool(branch)

        with scope("f_wait2"):

            @pl.when(jnp.logical_not(first))
            def _():
                f_copy(m, NC).wait_recv()

        low1 = g1 * inp[m] + pool_branch
        outp[m] = low1
        pooled = (low1 * 0.25).astype(bf16)
        pooled_s[m] = pooled
        grown = [dot(pooled, down[:, a:b]) for a, b in cuts]
        for k, (a, b) in enumerate(cuts):
            lifted, slope2 = gelu_pair(grown[k])
            slope2_s[m, k, :, 0 : b - a] = slope2
            out2[m, k, :, 0 : b - a] = g2[:, a:b] * in2[m, k, :, 0 : b - a] + lifted

            @pl.when(jnp.logical_not(last))
            def _():
                f_copy(m, k).start()

        @pl.when(jnp.logical_not(last))
        def _():
            f_copy(m, NC).start()

        return carry

    with scope("FWD"):
        lax.fori_loop(0, M, forward, 0)

    def full_state(m):
        for r in range(3):

            @pl.when(jnp.logical_not(first))
            def _():
                f_row(m, r).wait_recv()

            out1[m, r] = g1 * in1[m, r] + branch_s[m, r]

            @pl.when(jnp.logical_not(last))
            def _():
                f_row(m, r).start()

    def g_copy(k, m, sk):
        return remote(
            gs_send.at[k, m], gs_recv.at[sk, m], g_ss.at[k, m], g_rs.at[sk, m], {"col": k}
        )

    def stem_out(m, low, high):
        for k in range(S):

            @pl.when((col != k) & (k >= col + low) & (k < col + high))
            def _():
                g_copy(k, m, col).start()

    n = D * T
    flat = lambda ref: ref[...].reshape(-1, ref.shape[-1])
    accs, gots = (acc_d, acc_m, acc_u), (got_d, got_m, got_u)
    fxs, fys = (fx_d, fx_m, fx_u), (fy_d, fy_m, fy_u)
    gxs, gys = (gx_d, gx_m, gx_u), (gy_d, gy_m, gy_u)

    def chunked():
        pick = spread(C1, D, T)
        hidden_c[...] = dot(flat(hidden_s), pick).astype(bf16)
        pooled_c[...] = dot(flat(pooled_s), pick).astype(bf16)
        narrow_c[...] = dot(flat(narrow_s), spread(C2, D, T)).astype(bf16)

    partner = {"dp": dp + 1 - 2 * par}

    def p_copy(i, q):
        return remote(
            accs[i].at[q, 1 - par], gots[i].at[q], p_ss.at[i, q], p_rs.at[i, q], partner
        )

    def x1_copy(i, q, sq):
        return remote(
            accs[i].at[q, par, 0], fxs[i].at[sq], x1_ss.at[i, q], x1_rs.at[i, sq],
            {"dp": 2 * q + par},
        )

    def y1_copy(i, q, h, sh):
        return remote(
            accs[i].at[q, par, 1, h], fys[i].at[sh, q], y1_ss.at[i, h, q], y1_rs.at[i, sh, q],
            {"strip": h},
        )

    def x2_copy(i, q, sq):
        return remote(
            accs[i].at[q, par, 1, strip], gxs[i].at[sq], x2_ss.at[i, q], x2_rs.at[i, sq],
            {"dp": 2 * q + par},
        )

    def y2_copy(i, h, sh):
        return remote(
            accs[i].at[mine, par, 0, h], gys[i].at[sh], y2_ss.at[i, h], y2_rs.at[i, sh],
            {"strip": h},
        )

    def store_grad(i, left, right):
        accs[i][...] = dot_outer(left[...], flat(right)).reshape(accs[i].shape)
        for q in range(Q):
            p_copy(i, q).start()

    def others(count, me, act):
        for t in range(count):

            @pl.when(me != t)
            def _():
                act(t)

    def join_pair(i):
        with scope("w_pair"):
            for q in range(Q):
                p_copy(i, q).wait_recv()
                accs[i][q, par] += gots[i][q]
            others(Q, mine, lambda q: x1_copy(i, q, mine).start())

        def send_y(h):
            for q in range(Q):
                y1_copy(i, q, h, strip).start()

        others(T, strip, send_y)

    def head(m):
        with scope("h_state"):
            full_state(m)
            for h in range(T):

                @pl.when(strip != h)
                def _():
                    lab_copy(h, m, h).wait_recv()

        rest = [out1[m, r] for r in range(3)]
        state = jnp.concatenate([outp[m] - (rest[0] + rest[1] + rest[2])] + rest, axis=0)
        wide2 = None
        for k, (a, b) in enumerate(cuts):
            part = dot(out2[m, k, :, 0 : b - a].astype(bf16), lat2[a:b])
            wide2 = part if wide2 is None else wide2 + part
        lateral = dot(state.astype(bf16), lat1[...])
        lateral = jnp.concatenate(
            [lateral[at : at + small] + wide2 for at in range(0, pix, small)], axis=0
        )
        active, slope = gelu_pair(lateral)
        logits = dot_back(active.astype(bf16), cls[...])
        shifted = jnp.exp(logits - jnp.max(logits, axis=-1, keepdims=True))
        probs = shifted / jnp.sum(shifted, axis=-1, keepdims=True)
        lane = lax.broadcasted_iota(jnp.int32, (wide, W), 1)
        line = lax.broadcasted_iota(jnp.int32, (wide, W), 0)
        found = []
        for ri in range(2):
            for ci in range(2):
                for h in range(T):
                    block = lab_full[m, h].astype(f32)
                    for row in range(rl // 2):
                        r = 2 * row + ri
                        turned = jnp.where(lane == 2 * line + ci, block[r : r + 1], 0.0)
                        found.append(jnp.sum(turned, axis=1, keepdims=True))
        label = jnp.concatenate(found, axis=0).astype(jnp.int32)
        onehot = (lax.broadcasted_iota(jnp.int32, logits.shape, 1) == label).astype(f32)
        grad_logits = (probs - onehot) * (loss_scale / npix)
        grad_lat = dot(grad_logits.astype(bf16), cls[...]) * slope
        cot1 = dot_back(grad_lat.astype(bf16), lat1[...])
        cinp[m] = cot1[0:small]
        for r in range(3):
            cin1[m, r] = cot1[(r + 1) * small :][:small] - cot1[0:small]
        pooled_lat = pool(grad_lat).astype(bf16)
        for k, (a, b) in enumerate(cuts):
            cin2[m, k, :, 0 : b - a] = dot_back(pooled_lat, lat2[a:b])

    def backward(m, carry):
        final = first & (m == M - 1)

        @pl.when(last)
        def _():
            with scope("HEAD"):
                head(m)

        with scope("b_rows"):
            for r in range(3):

                @pl.when(jnp.logical_not(last))
                def _():
                    b_row(m, r).wait_recv()

                @pl.when(jnp.logical_not(first))
                def _():
                    cout1[m, r] = g1 * cin1[m, r]
                    b_row(m, r).start()

        risen = None
        for k, (a, b) in enumerate(cuts):
            with scope("b_wait1"):

                @pl.when(jnp.logical_not(last))
                def _():
                    b_copy(m, k).wait_recv()

            lift = (cin2[m, k, :, 0 : b - a] * slope2_s[m, k, :, 0 : b - a]).astype(bf16)
            lift_s[m, :, a:b] = lift
            part = dot_back(lift, down[:, a:b])
            risen = part if risen is None else risen + part

        with scope("b_wait2"):

            @pl.when(jnp.logical_not(last))
            def _():
                b_copy(m, NC).wait_recv()

        low = cinp[m] + risen * 0.25

        @pl.when(jnp.logical_not(first))
        def _():
            coutp[m] = g1 * low
            b_copy(m, NC).start()

        total = jnp.concatenate([low] + [low + cin1[m, r] for r in range(3)], axis=0)
        total_narrow = total.astype(bf16)
        total_s[m] = total_narrow

        @pl.when(final)
        def _():
            store_grad(0, pooled_c, lift_s)

        grad_depth = dot_back(total_narrow, mix[...]) * slope1_s[m]
        grad_mixture = depthwise(grad_depth, -1)
        grad_narrow = pool(grad_mixture).astype(bf16)
        gnar_s[m] = grad_narrow

        @pl.when(jnp.logical_not(first))
        def _():
            for k, (a, b) in enumerate(cuts):
                cout2[m, k, :, 0 : b - a] = g2[:, a:b] * cin2[m, k, :, 0 : b - a] + dot_back(
                    grad_narrow, up[a:b]
                )
                with scope("b_send1"):
                    b_copy(m, k).start()

        @pl.when(final)
        def _():
            join_pair(0)
            store_grad(2, narrow_c, gnar_s)
            store_grad(1, hidden_c, total_s)

        parts = split(grad_mixture)
        for ri in range(2):
            for ci in range(2):
                for row in range(rows // 2):
                    for at, (a, b) in enumerate(lanes):
                        natural[at, 2 * row + ri, pl.ds(ci, wide, stride=2), 0 : b - a] = parts[
                            ri
                        ][ci][row * wide : (row + 1) * wide, a:b]
        for k in range(S):
            for h in range(T):
                for at, (a, b) in enumerate(lanes):
                    gs_send[k, m, h, :, :, a:b] = natural[
                        at, h * rl : (h + 1) * rl, k * wc : (k + 1) * wc, 0 : b - a
                    ]
        for k in range(S):

            @pl.when(col == k)
            def _():
                gs_recv[k, m] = gs_send[k, m]

        @pl.when(first)
        def _():
            stem_out(m, 1, S)

        for t, line in enumerate(tap_sums(mixture_s[m], grad_depth)):
            gk[t : t + 1] += line
        return carry

    @pl.when(jnp.logical_not(last))
    def _():
        chunked()
        with scope("fullstate"):
            for m in range(M):
                full_state(m)

    @pl.when(last)
    def _():
        for load in loads[4:]:
            load.wait()

    with scope("BWD"):
        lax.fori_loop(0, M, backward, 0)

    @pl.when(last)
    def _():
        chunked()

    @pl.when(jnp.logical_not(first))
    def _():
        for m in range(M):
            stem_out(m, 1, S)

    def k_copy(stage, src, dst, target, t, st):
        return remote(src, dst, k_ss.at[stage, t], k_rs.at[stage, st], target)

    def kp():
        return k_copy(0, gk, gk_got, partner, 0, 0)

    def kx(q, sq):
        return k_copy(1, gk_pair, gk_x.at[sq], {"dp": 2 * q + par}, q, sq)

    def ky(h, sh):
        return k_copy(2, gk_sum, gk_y.at[sh], {"strip": h}, h, sh)

    kp().start()

    @pl.when(jnp.logical_not(first))
    def _():
        store_grad(0, pooled_c, lift_s)
        store_grad(1, hidden_c, total_s)
        store_grad(2, narrow_c, gnar_s)
        join_pair(0)

    kp().wait_recv()
    gk_pair[...] = gk[...] + gk_got[...]
    others(Q, mine, lambda q: kx(q, mine).start())
    join_pair(2)
    join_pair(1)

    @pl.when(jnp.logical_not(first))
    def _():
        for m in range(M):
            stem_out(m, -1, 0)

    gk_sum[...] = gk_pair[...]

    def add_kx(q):
        kx(q, q).wait_recv()
        gk_sum[...] += gk_x[q]

    others(Q, mine, add_kx)
    others(T, strip, lambda h: ky(h, strip).start())

    def gy_copy(h, sh):
        return remote(
            stem_sum.at[h], stem_far.at[sh], gy_ss.at[h], gy_rs.at[sh], {"strip": h}
        )

    def stem_total():
        def landed(k):
            for m in range(M):
                g_copy(k, m, k).wait_recv()

        others(S, col, landed)
        for h in range(T):
            for m in range(M):
                total = gs_recv[0, m, h]
                for k in range(1, S):
                    total = total + gs_recv[k, m, h]
                stem_sum[h, m] = total
        others(T, strip, lambda h: gy_copy(h, strip).start())

    with scope("w_stem1"):
        pl.when(first)(stem_total)

    for i in (0, 2, 1):

        def add_x(q):
            x1_copy(i, q, q).wait_recv()
            accs[i][mine, par, 0] += fxs[i][q]

        with scope("w_addx"):
            others(Q, mine, add_x)
            others(T, strip, lambda h: y2_copy(i, h, strip).start())

        def add_y(h):
            for q in range(Q):
                y1_copy(i, q, h, h).wait_recv()
                accs[i][q, par, 1, strip] += fys[i][h, q]

        with scope("w_addy"):
            others(T, strip, add_y)
            others(Q, mine, lambda q: x2_copy(i, q, mine).start())

    @pl.when(jnp.logical_not(first))
    def _():
        with scope("w_stem2"):
            for m in range(M):
                stem_out(m, -S, -1)
            stem_total()

    def add_ky(h):
        ky(h, h).wait_recv()

    others(T, strip, add_ky)
    share_k = gk_sum[...]
    for h in range(T):
        share_k = share_k + jnp.where(strip != h, gk_y[h], 0.0)
    w = C1 // n
    share = share_k[0:9, 0:w]
    for k in range(1, n):
        share = jnp.where(dp * T + strip == k, share_k[0:9, k * w : (k + 1) * w], share)
    o_taps[...] = share

    for i, out in ((0, o_down), (2, o_up), (1, o_mix)):

        def last_y(h):
            y2_copy(i, h, h).wait_recv()
            accs[i][mine, par, 0, strip] += gys[i][h]

        with scope("w_lasty"):
            others(T, strip, last_y)

        def last_x(q):
            x2_copy(i, q, q).wait_recv()
            accs[i][mine, par, 1, strip] += gxs[i][q]

        with scope("w_lastx"):
            others(Q, mine, last_x)
        half = accs[i].shape[4]
        out[0:half] = accs[i][mine, par, 0, strip]
        out[half:] = accs[i][mine, par, 1, strip][0 : out.shape[0] - half]

    for h in range(T):
        rows_h = slice(h * M, (h + 1) * M)

        @pl.when(strip == h)
        def _():
            o_stem[rows_h] = stem_sum[h]

        @pl.when(strip != h)
        def _():
            gy_copy(h, h).wait_recv()
            o_stem[rows_h] = stem_far[h]

    for m in range(M):
        for h in range(T):

            @pl.when(strip != h)
            def _():
                stem_copy(h, m, strip).wait_send()
                lab_copy(h, m, strip).wait_send()

                @pl.when(jnp.logical_not(last))
                def _():
                    lab_copy(h, m, h).wait_recv()

        @pl.when(jnp.logical_not(last))
        def _():
            for k in range(NC + 1):
                f_copy(m, k).wait_send()
            for r in range(3):
                f_row(m, r).wait_send()

        @pl.when(jnp.logical_not(first))
        def _():
            for k in range(NC + 1):
                b_copy(m, k).wait_send()
            for r in range(3):
                b_row(m, r).wait_send()

    def sent_stem(k):
        for m in range(M):
            g_copy(k, m, col).wait_send()

    others(S, col, sent_stem)
    others(T, strip, lambda h: gy_copy(h, strip).wait_send())
    kp().wait_send()
    others(Q, mine, lambda q: kx(q, mine).wait_send())
    others(T, strip, lambda h: ky(h, strip).wait_send())
    for i in range(3):
        for q in range(Q):
            p_copy(i, q).wait_send()

        def sent_x(q):
            x1_copy(i, q, mine).wait_send()
            x2_copy(i, q, mine).wait_send()

        def sent_y(h):
            for q in range(Q):
                y1_copy(i, q, h, strip).wait_send()
            y2_copy(i, h, strip).wait_send()

        others(Q, mine, sent_x)
        others(T, strip, sent_y)


def finish(*refs):
    for source, target in zip(refs[:4], refs[5:9]):
        target[...] = source[...].reshape(target.shape)
    refs[9][...] = refs[4][...]


def shards(stem, labels, up, mix, down, taps, gain1, gain2, lat1, lat2, cls):
    B, rl, W, C1 = stem.shape
    C2 = up.shape[1]
    S, D, T = lax.axis_size("col"), lax.axis_size("dp"), lax.axis_size("strip")
    M = B // T
    RW = rl * W
    pix = T * RW
    small = pix // 4
    wc = W // S
    n = D * T
    Q = D // 2
    p1, p2 = up_to(C1 // n, 16), up_to(C2 // n, 16)
    halves = ((p1 // 2, C2), (p1 // 2, C1), (p2 // 2, C1))
    step = 256
    cuts = tuple((a, min(a + step, C2)) for a in range(0, C2, step))
    NC = len(cuts)
    npix = float(B * D * rl * T * W)
    V = pltpu.VMEM
    dma = pltpu.SemaphoreType.DMA
    vspec = pl.BlockSpec(memory_space=pltpu.VMEM)
    hspec = pl.BlockSpec(memory_space=pltpu.HBM)
    held = [stem.reshape(B, RW, C1), up[0], mix[0], down[0], lat1, lat2]
    outs = pl.pallas_call(
        functools.partial(kernel, S, D, T, M, rl, W, npix, cuts),
        out_shape=(
            jax.ShapeDtypeStruct((C2 // n, C1), f32),
            jax.ShapeDtypeStruct((C1 // n, C1), f32),
            jax.ShapeDtypeStruct((C1 // n, C2), f32),
            jax.ShapeDtypeStruct((9, C1 // n), f32),
            jax.ShapeDtypeStruct((B, rl, wc, C1), f32),
        ),
        in_specs=[hspec] * 6 + [vspec] * 5,
        out_specs=(vspec,) * 5,
        scratch_shapes=[
            *[V(a.shape, bf16) for a in held],
            V((T, M, 4, RW // 4, C1), f32),
            V((M, 4, T, RW // 4, C1), f32),
            V((M, T, rl, W), jnp.int32),
            V((M, 3, small, C1), f32),
            V((M, NC, small, step), f32),
            V((M, 3, small, C1), f32),
            V((M, NC, small, step), f32),
            V((M, 3, small, C1), f32),
            V((M, NC, small, step), f32),
            V((M, 3, small, C1), f32),
            V((M, NC, small, step), f32),
            V((M, small, C1), f32),
            V((M, small, C1), f32),
            V((M, small, C1), f32),
            V((M, small, C1), f32),
            V((M, 3, small, C1), f32),
            V((M * pix, n * p1), bf16),
            V((M * small, n * p1), bf16),
            V((M * small, n * p2), bf16),
            V((M, pix, C1), f32),
            V((M, pix, C1), f32),
            V((M, pix, C1), bf16),
            V((M, small, C2), bf16),
            V((M, small, C1), bf16),
            V((M, NC, small, step), f32),
            V((M, pix, C1), bf16),
            V((M, small, C2), bf16),
            V((M, small, C1), bf16),
            V((up_to(C1, 128) // 128, T * rl, W, 128), f32),
            V((S, M, T, rl, wc, C1), f32),
            V((S, M, T, rl, wc, C1), f32),
            V((T, M, rl, wc, C1), f32),
            V((T, M, rl, wc, C1), f32),
            *[V((Q, 2, 2, T, h, c), f32) for h, c in halves],
            *[V((Q, 2, T, h, c), f32) for h, c in halves],
            *[V((Q, T, h, c), f32) for h, c in halves],
            *[V((T, Q, h, c), f32) for h, c in halves],
            *[V((Q, h, c), f32) for h, c in halves],
            *[V((T, h, c), f32) for h, c in halves],
            V((16, C1), f32),
            V((16, C1), f32),
            V((16, C1), f32),
            V((Q, 16, C1), f32),
            V((16, C1), f32),
            V((T, 16, C1), f32),
            dma((6,)),
            dma((T, M)),
            dma((T, M)),
            dma((T, M)),
            dma((T, M)),
            dma((M, NC + 1)),
            dma((M, NC + 1)),
            dma((M, NC + 1)),
            dma((M, NC + 1)),
            dma((S, M)),
            dma((S, M)),
            dma((T,)),
            dma((T,)),
            dma((3, Q)),
            dma((3, Q)),
            dma((3, Q)),
            dma((3, Q)),
            dma((3, T, Q)),
            dma((3, T, Q)),
            dma((3, Q)),
            dma((3, Q)),
            dma((3, T)),
            dma((3, T)),
            dma((3, max(Q, T))),
            dma((3, max(Q, T))),
            dma((M, 3)),
            dma((M, 3)),
            dma((M, 3)),
            dma((M, 3)),
        ],
        compiler_params=pltpu.CompilerParams(
            collective_id=0, has_side_effects=True, vmem_limit_bytes=60000 * 1024
        ),
        name="columns",
    )(*held, cls.T, labels, taps[0], gain1, gain2)
    tall = lambda a: jax.ShapeDtypeStruct((a.shape[0], 1, a.shape[1]), f32)
    done = pl.pallas_call(
        finish,
        out_shape=tuple(tall(a) for a in outs[:4])
        + (jax.ShapeDtypeStruct(outs[4].shape, f32),),
        in_specs=[vspec] * 5,
        out_specs=(vspec,) * 5,
        name="finish",
    )(*outs)
    return tuple(jnp.transpose(a, (1, 0, 2)) for a in done[:4]) + (done[4],)


def solution(mesh):
    placed = (
        P("dp", "strip", None, None),
        P("dp", "strip", None),
        P("col", None, None),
        P("col", None, None),
        P("col", None, None),
        P("col", None, None),
        P("col", None),
        P("col", None),
        P(),
        P(),
        P(),
    )
    return jax.shard_map(
        shards,
        mesh=mesh,
        in_specs=placed,
        out_specs=(
            P("col", ("dp", "strip"), None),
            P("col", ("dp", "strip"), None),
            P("col", ("dp", "strip"), None),
            P("col", None, ("dp", "strip")),
            P("dp", "strip", "col", None),
        ),
        check_vma=False,
    )
```

```python
import contextlib
import functools

import jax
import jax.numpy as jnp
from jax import lax
from jax.experimental import pallas as pl
from jax.experimental.pallas import tpu as pltpu
from jax.sharding import PartitionSpec as P

loss_scale = 64.0
root_coef = 0.7978845608028654
cube_coef = 0.044715
f32 = jnp.float32
bf16 = jnp.bfloat16
MESH = pl.DeviceIdType.MESH
scope = contextlib.nullcontext


def gelu_pair(values):
    square = values * values
    tangent = jnp.tanh(root_coef * (values + cube_coef * values * square))
    half = 0.5 * (1.0 + tangent)
    slope = half + 0.5 * values * (1.0 - tangent * tangent) * root_coef * (
        1.0 + 3.0 * cube_coef * square
    )
    return values * half, slope


def dot(left, right):
    return jnp.dot(left, right, preferred_element_type=f32)


def dot_back(left, right):
    return lax.dot_general(left, right, (((1,), (1,)), ((), ())), preferred_element_type=f32)


def dot_outer(left, right):
    return lax.dot_general(left, right, (((0,), (0,)), ((), ())), preferred_element_type=f32)


def up_to(count, multiple):
    return -(-count // multiple) * multiple


def spread(count, owners, T):
    parts = owners * T
    run = count // parts
    half = up_to(run, 16) // 2
    source = lax.broadcasted_iota(jnp.int32, (count, 1), 0)
    target = source
    before = 0
    for owner in range(owners):
        for h in range(T):
            for side in range(2):
                begin = (owner * T + h) * run + side * half
                place = (owner % 2) * (owners // 2) + owner // 2
                shift = ((place * 2 + side) * T + h) * half - begin
                target = target + jnp.where(source >= begin, shift - before, 0)
                before = shift
    spot = lax.broadcasted_iota(jnp.int32, (count, parts * 2 * half), 1)
    return (spot == target).astype(f32).astype(bf16)


def phase_matrix(rl, W):
    count, wide, quarter = rl * W, W // 2, rl * W // 4
    out = lax.broadcasted_iota(jnp.int32, (count, count), 0)
    source = lax.broadcasted_iota(jnp.int32, (count, count), 1)
    hit = jnp.zeros((count, count), jnp.bool_)
    for ri in range(2):
        for ci in range(2):
            for row in range(rl // 2):
                rest = out - ((2 * ri + ci) * quarter + row * wide)
                inside = (rest >= 0) & (rest < wide)
                hit = hit | (inside & (source == (2 * row + ri) * W + ci + 2 * rest))
    return hit.astype(f32).astype(bf16)


def kernel(
    S, D, T, M, rl, W, npix, cuts,
    stem_h, up_h, mix_h, down_h, taps_h, gain1_h, gain2_h, labels_h, lat1_h, lat2_h, cls_h,
    o_up, o_mix, o_down, o_taps, o_stem,
    h_up, h_mix, h_down, h_taps,
    stem, up, mix, down, taps, gain1, gain2, labels, lat1, lat2, cls,
    stem_send, stem_full, lab_full, in1, in2, out1, out2, cin1, cin2, cout1, cout2,
    inp, outp, cinp, coutp, branch_s, hidden_c, pooled_c, narrow_c,
    grad_depth_s, grad_mixture_s, mixture_s, slope1_s, hidden_s, narrow_s, pooled_s, slope2_s, total_s, lift_s, gnar_s,
    natural, gs_send, gs_recv, stem_sum, stem_far,
    acc_d, acc_m, acc_u, got_d, got_m, got_u, fx_d, fx_m, fx_u, fy_d, fy_m, fy_u,
    gx_d, gx_m, gx_u, gy_d, gy_m, gy_u, gk, gk_got, gk_pair, gk_x, gk_sum, gk_y,
    load_s,
    stem_ss, stem_rs, lab_ss, lab_rs, f_ss, f_rs, g_ss, g_rs, gy_ss, gy_rs,
    p_ss, p_rs, x1_ss, x1_rs, y1_ss, y1_rs, x2_ss, x2_rs, y2_ss, y2_rs,
    k_ss, k_rs, ff_ss, ff_rs,
):
    col, dp, strip = lax.axis_index("col"), lax.axis_index("dp"), lax.axis_index("strip")
    first, last = col == 0, col == S - 1
    C1, C2 = up.shape[1], up.shape[0]
    pix = T * rl * W
    small = pix // 4
    rows = T * rl
    wide = W // 2
    wc = W // S
    NC = len(cuts)
    lanes = [(a, min(a + 128, C1)) for a in range(0, C1, 128)]
    par = lax.rem(dp, 2)
    mine = dp // 2
    Q = D // 2

    def remote(src, dst, ss, rs, target):
        return pltpu.make_async_remote_copy(
            src_ref=src, dst_ref=dst, send_sem=ss, recv_sem=rs,
            device_id=target, device_id_type=MESH,
        )

    gate = pltpu.get_barrier_semaphore()
    for h in range(T):
        for k in range(S):

            @pl.when((col != k) | (strip != h))
            def _():
                pl.semaphore_signal(
                    gate, inc=1, device_id={"col": k, "strip": h}, device_id_type=MESH
                )

        for d in range(D):

            @pl.when(dp != d)
            def _():
                pl.semaphore_signal(
                    gate, inc=1, device_id={"dp": d, "strip": h}, device_id_type=MESH
                )

    loads = [
        pltpu.make_async_copy(src, dst, load_s.at[i])
        for i, (src, dst) in enumerate(
            ((stem_h, stem), (up_h, up), (mix_h, mix), (down_h, down),
             (taps_h, taps), (gain1_h, gain1), (gain2_h, gain2), (labels_h, labels),
             (lat1_h, lat1), (lat2_h, lat2), (cls_h, cls))
        )
    ]
    for load in loads[:8]:
        load.start()

    @pl.when(last)
    def _():
        for load in loads[8:]:
            load.start()

    @pl.when(first)
    def _():
        in2[...] = jnp.zeros_like(in2)
        in1[...] = jnp.zeros_like(in1)
        inp[...] = jnp.zeros_like(inp)

    gk[...] = jnp.zeros_like(gk)
    order = phase_matrix(rl, W)
    loads[0].wait()
    for m in range(M):
        for h in range(T):
            stem_send[h, m] = dot(order, stem[h * M + m]).reshape(stem_send.shape[2:])
    for load in loads[1:8]:
        load.wait()
    with scope("gatewait"):
        pl.semaphore_wait(gate, S * T - 1 + (D - 1) * T)

    def stem_copy(h, m, slot):
        return remote(
            stem_send.at[h, m], stem_full.at[m, :, slot], stem_ss.at[h, m], stem_rs.at[slot, m],
            {"strip": h},
        )

    def lab_copy(h, m, slot):
        return remote(
            labels.at[h * M + m], lab_full.at[m, slot], lab_ss.at[h, m], lab_rs.at[slot, m],
            {"strip": h},
        )

    for m in range(M):
        for h in range(T):

            @pl.when(strip != h)
            def _():
                stem_copy(h, m, strip).start()

    for m in range(M):
        for h in range(T):

            @pl.when(strip != h)
            def _():
                lab_copy(h, m, strip).start()

            @pl.when(strip == h)
            def _():
                stem_full[m, :, h] = stem_send[h, m]
                lab_full[m, h] = labels[h * M + m]

    kern = taps[0:9].astype(f32)
    g1 = gain1[...]
    g2 = gain2[...]
    place = lax.rem(lax.broadcasted_iota(jnp.int32, (small, 1), 0), wide)
    not_low = place != 0
    not_high = place != wide - 1

    def split(values):
        return [[values[(2 * ri + ci) * small :][:small] for ci in range(2)] for ri in range(2)]

    def join(parts):
        return jnp.concatenate([parts[ri][ci] for ri in range(2) for ci in range(2)], axis=0)

    def pool(values):
        return (values[0:small] + values[small : 2 * small]) + (
            values[2 * small : 3 * small] + values[3 * small :]
        )

    def sources(parts):
        found = []
        for ri in range(2):
            even, odd = parts[ri]
            before = jnp.where(not_low, pltpu.roll(odd, 1, 0), 0.0)
            after = jnp.where(not_high, pltpu.roll(even, small - 1, 0), 0.0)
            found.append(((before, even, odd), (even, odd, after)))
        return found

    def rows_moved(values, step):
        if step == 0:
            return values
        blank = jnp.zeros((wide, values.shape[1]), f32)
        if step > 0:
            return jnp.concatenate([values[wide:], blank], axis=0)
        return jnp.concatenate([blank, values[:-wide]], axis=0)

    def depthwise(values, sign):
        found = sources(split(values))
        parts = [[None, None], [None, None]]
        for ri in range(2):
            for ci in range(2):
                total = None
                for i in (-1, 0, 1):
                    line = None
                    for j in (-1, 0, 1):
                        t = 3 * (sign * i + 1) + (sign * j + 1)
                        term = kern[t : t + 1] * found[(ri + i) % 2][ci][j + 1]
                        line = term if line is None else line + term
                    line = rows_moved(line, (ri + i) // 2)
                    total = line if total is None else total + line
                parts[ri][ci] = total
        return join(parts)

    def tap_sums(values, grads):
        found, grads = sources(split(values)), split(grads)
        lines = []
        for i in (-1, 0, 1):
            for j in (-1, 0, 1):
                total = None
                for ri in range(2):
                    for ci in range(2):
                        window, grad = found[(ri + i) % 2][ci][j + 1], grads[ri][ci]
                        step = (ri + i) // 2
                        if step > 0:
                            window, grad = window[wide:], grad[:-wide]
                        elif step < 0:
                            window, grad = window[:-wide], grad[wide:]
                        both = window * grad
                        for at in range(0, both.shape[0], wide):
                            piece = both[at : at + wide]
                            total = piece if total is None else total + piece
                lines.append(jnp.sum(total, axis=0, keepdims=True))
        return lines

    def f_copy(m, k):
        src, dst = (out2.at[m, k], in2.at[m, k]) if k < NC else (outp.at[m], inp.at[m])
        return remote(src, dst, f_ss.at[m, k], f_rs.at[m, k], {"col": col + 1})

    def b_copy(m, k):
        src, dst = (cout2.at[m, k], cin2.at[m, k]) if k < NC else (coutp.at[m], cinp.at[m])
        return remote(src, dst, f_ss.at[m, k], f_rs.at[m, k], {"col": col - 1})

    def f_row(m, r):
        return remote(
            out1.at[m, r], in1.at[m, r], ff_ss.at[m, r], ff_rs.at[m, r], {"col": col + 1}
        )

    def b_row(m, r):
        return remote(
            cout1.at[m, r], cin1.at[m, r], ff_ss.at[m, r], ff_rs.at[m, r], {"col": col - 1}
        )

    def forward(m, carry):
        with scope("f_stemwait"):
            for h in range(T):

                @pl.when(strip != h)
                def _():
                    stem_copy(h, m, h).wait_recv()

        risen = None
        for k, (a, b) in enumerate(cuts):
            with scope("f_wait1"):

                @pl.when(jnp.logical_not(first))
                def _():
                    f_copy(m, k).wait_recv()

            narrow = in2[m, k, :, 0 : b - a].astype(bf16)
            narrow_s[m, :, a:b] = narrow
            part = dot(narrow, up[a:b])
            risen = part if risen is None else risen + part
        mixture = stem_full[m].reshape(pix, C1) + jnp.concatenate([risen] * 4, axis=0)
        mixture_s[m] = mixture
        active, slope = gelu_pair(depthwise(mixture, 1))
        slope1_s[m] = slope
        hidden = active.astype(bf16)
        hidden_s[m] = hidden
        branch = dot(hidden, mix[...])
        branch_s[m] = branch[small:].reshape(branch_s.shape[1:])
        pool_branch = pool(branch)

        with scope("f_wait2"):

            @pl.when(jnp.logical_not(first))
            def _():
                f_copy(m, NC).wait_recv()

        low1 = g1 * inp[m] + pool_branch
        outp[m] = low1
        pooled = (low1 * 0.25).astype(bf16)
        pooled_s[m] = pooled
        grown = [dot(pooled, down[:, a:b]) for a, b in cuts]
        for k, (a, b) in enumerate(cuts):
            lifted, slope2 = gelu_pair(grown[k])
            slope2_s[m, k, :, 0 : b - a] = slope2
            out2[m, k, :, 0 : b - a] = g2[:, a:b] * in2[m, k, :, 0 : b - a] + lifted

            @pl.when(jnp.logical_not(last))
            def _():
                f_copy(m, k).start()

        @pl.when(jnp.logical_not(last))
        def _():
            f_copy(m, NC).start()

        return carry

    with scope("FWD"):
        lax.fori_loop(0, M, forward, 0)

    def full_state(m):
        for r in range(3):

            @pl.when(jnp.logical_not(first))
            def _():
                f_row(m, r).wait_recv()

            out1[m, r] = g1 * in1[m, r] + branch_s[m, r]

            @pl.when(jnp.logical_not(last))
            def _():
                f_row(m, r).start()

    def g_copy(k, sk):
        return remote(gs_send.at[k], gs_recv.at[sk], g_ss.at[k], g_rs.at[sk], {"col": k})

    def stem_out(low, high):
        for k in range(S):

            @pl.when((col != k) & (k >= col + low) & (k < col + high))
            def _():
                g_copy(k, col).start()

    n = D * T
    flat = lambda ref: ref[...].reshape(-1, ref.shape[-1])
    accs, gots = (acc_d, acc_m, acc_u), (got_d, got_m, got_u)
    fxs, fys = (fx_d, fx_m, fx_u), (fy_d, fy_m, fy_u)
    gxs, gys = (gx_d, gx_m, gx_u), (gy_d, gy_m, gy_u)

    def chunked():
        pick = spread(C1, D, T)
        hidden_c[...] = dot(flat(hidden_s), pick).astype(bf16)
        pooled_c[...] = dot(flat(pooled_s), pick).astype(bf16)
        narrow_c[...] = dot(flat(narrow_s), spread(C2, D, T)).astype(bf16)

    partner = {"dp": dp + 1 - 2 * par}

    def rel(a, b, count):
        return 0 if count == 2 else lax.rem(a - b - 1 + count, count)

    def ends(other, source, me, count):
        back = rel(me, other, count) if source is me else rel(other, me, count)
        return rel(other, me, count), back

    def p_copy(i):
        return remote(accs[i].at[1 - par], gots[i], p_ss.at[i], p_rs.at[i], partner)

    def x1_copy(i, q, sq):
        a, b = ends(q, sq, mine, Q)
        return remote(
            accs[i].at[par, q, 0], fxs[i].at[sq], x1_ss.at[i, a], x1_rs.at[i, b],
            {"dp": 2 * q + par},
        )

    def y1_copy(i, h, sh):
        a, b = ends(h, sh, strip, T)
        return remote(
            accs[i].at[par, :, 1, h], fys[i].at[sh], y1_ss.at[i, a], y1_rs.at[i, b],
            {"strip": h},
        )

    def x2_copy(i, q, sq):
        a, b = ends(q, sq, mine, Q)
        return remote(
            accs[i].at[par, q, 1, strip], gxs[i].at[sq], x2_ss.at[i, a], x2_rs.at[i, b],
            {"dp": 2 * q + par},
        )

    def y2_copy(i, h, sh):
        a, b = ends(h, sh, strip, T)
        return remote(
            accs[i].at[par, mine, 0, h], gys[i].at[sh], y2_ss.at[i, a], y2_rs.at[i, b],
            {"strip": h},
        )

    def store_grad(i, left, right):
        accs[i][...] = dot_outer(left[...], flat(right)).reshape(accs[i].shape)
        p_copy(i).start()

    def others(count, me, act):
        for t in range(count):

            @pl.when(me != t)
            def _():
                act(t)

    def join_pair(i):
        with scope("w_pair"):
            p_copy(i).wait_recv()
            accs[i][par] += gots[i][...]
            others(Q, mine, lambda q: x1_copy(i, q, mine).start())

        others(T, strip, lambda h: y1_copy(i, h, strip).start())

    def head(m):
        with scope("h_state"):
            full_state(m)
            for h in range(T):

                @pl.when(strip != h)
                def _():
                    lab_copy(h, m, h).wait_recv()

        rest = [out1[m, r] for r in range(3)]
        state = jnp.concatenate([outp[m] - (rest[0] + rest[1] + rest[2])] + rest, axis=0)
        wide2 = None
        for k, (a, b) in enumerate(cuts):
            part = dot(out2[m, k, :, 0 : b - a].astype(bf16), lat2[a:b])
            wide2 = part if wide2 is None else wide2 + part
        lateral = dot(state.astype(bf16), lat1[...])
        lateral = jnp.concatenate(
            [lateral[at : at + small] + wide2 for at in range(0, pix, small)], axis=0
        )
        active, slope = gelu_pair(lateral)
        logits = dot_back(active.astype(bf16), cls[...])
        shifted = jnp.exp(logits - jnp.max(logits, axis=-1, keepdims=True))
        probs = shifted / jnp.sum(shifted, axis=-1, keepdims=True)
        lane = lax.broadcasted_iota(jnp.int32, (wide, W), 1)
        line = lax.broadcasted_iota(jnp.int32, (wide, W), 0)
        found = []
        for ri in range(2):
            for ci in range(2):
                for h in range(T):
                    block = lab_full[m, h].astype(f32)
                    for row in range(rl // 2):
                        r = 2 * row + ri
                        turned = jnp.where(lane == 2 * line + ci, block[r : r + 1], 0.0)
                        found.append(jnp.sum(turned, axis=1, keepdims=True))
        label = jnp.concatenate(found, axis=0).astype(jnp.int32)
        onehot = (lax.broadcasted_iota(jnp.int32, logits.shape, 1) == label).astype(f32)
        grad_logits = (probs - onehot) * (loss_scale / npix)
        grad_lat = dot(grad_logits.astype(bf16), cls[...]) * slope
        cot1 = dot_back(grad_lat.astype(bf16), lat1[...])
        cinp[m] = cot1[0:small]
        for r in range(3):
            cin1[m, r] = cot1[(r + 1) * small :][:small] - cot1[0:small]
        pooled_lat = pool(grad_lat).astype(bf16)
        for k, (a, b) in enumerate(cuts):
            cin2[m, k, :, 0 : b - a] = dot_back(pooled_lat, lat2[a:b])

    def k_copy(stage, src, dst, target, t, st):
        return remote(src, dst, k_ss.at[stage, t], k_rs.at[stage, st], target)

    def kp():
        return k_copy(0, gk, gk_got, partner, 0, 0)

    def kx(q, sq):
        return k_copy(1, gk_pair, gk_x.at[sq], {"dp": 2 * q + par}, q, sq)

    def ky(h, sh):
        return k_copy(2, gk_sum, gk_y.at[sh], {"strip": h}, h, sh)

    def tap_part(m):
        for t, line in enumerate(tap_sums(mixture_s[m], grad_depth_s[m])):
            gk[t : t + 1] += line

    def stem_part(m):
        parts = split(grad_mixture_s[m])
        for ri in range(2):
            for ci in range(2):
                for row in range(rows // 2):
                    for at, (a, b) in enumerate(lanes):
                        natural[at, 2 * row + ri, pl.ds(ci, wide, stride=2), 0 : b - a] = parts[
                            ri
                        ][ci][row * wide : (row + 1) * wide, a:b]
        for k in range(S):
            for h in range(T):
                for at, (a, b) in enumerate(lanes):
                    gs_send[k, m, h, :, :, a:b] = natural[
                        at, h * rl : (h + 1) * rl, k * wc : (k + 1) * wc, 0 : b - a
                    ]
        for k in range(S):

            @pl.when(col == k)
            def _():
                gs_recv[k, m] = gs_send[k, m]

        @pl.when(first & (m == M - 1))
        def _():
            stem_out(1, S)

    def backward(m, carry):
        final = first & (m == M - 1)

        @pl.when(last)
        def _():
            with scope("HEAD"):
                head(m)

        with scope("b_rows"):
            for r in range(3):

                @pl.when(jnp.logical_not(last))
                def _():
                    b_row(m, r).wait_recv()

                @pl.when(jnp.logical_not(first))
                def _():
                    cout1[m, r] = g1 * cin1[m, r]
                    b_row(m, r).start()

        risen = None
        for k, (a, b) in enumerate(cuts):
            with scope("b_wait1"):

                @pl.when(jnp.logical_not(last))
                def _():
                    b_copy(m, k).wait_recv()

            lift = (cin2[m, k, :, 0 : b - a] * slope2_s[m, k, :, 0 : b - a]).astype(bf16)
            lift_s[m, :, a:b] = lift
            part = dot_back(lift, down[:, a:b])
            risen = part if risen is None else risen + part

        with scope("b_wait2"):

            @pl.when(jnp.logical_not(last))
            def _():
                b_copy(m, NC).wait_recv()

        low = cinp[m] + risen * 0.25

        @pl.when(jnp.logical_not(first))
        def _():
            coutp[m] = g1 * low
            b_copy(m, NC).start()

        total = jnp.concatenate([low] + [low + cin1[m, r] for r in range(3)], axis=0)
        total_narrow = total.astype(bf16)
        total_s[m] = total_narrow

        @pl.when(final)
        def _():
            store_grad(0, pooled_c, lift_s)

        grad_depth = dot_back(total_narrow, mix[...]) * slope1_s[m]
        grad_mixture = depthwise(grad_depth, -1)
        grad_narrow = pool(grad_mixture).astype(bf16)
        gnar_s[m] = grad_narrow

        @pl.when(jnp.logical_not(first))
        def _():
            for k, (a, b) in enumerate(cuts):
                cout2[m, k, :, 0 : b - a] = g2[:, a:b] * cin2[m, k, :, 0 : b - a] + dot_back(
                    grad_narrow, up[a:b]
                )
                with scope("b_send1"):
                    b_copy(m, k).start()

        grad_depth_s[m] = grad_depth
        grad_mixture_s[m] = grad_mixture

        @pl.when(final)
        def _():
            store_grad(2, narrow_c, gnar_s)
            store_grad(1, hidden_c, total_s)

        @pl.when(jnp.logical_not(last))
        def _():
            tap_part(m)

            @pl.when(final)
            def _():
                kp().start()
                join_pair(0)

            stem_part(m)

        return carry

    @pl.when(jnp.logical_not(last))
    def _():
        chunked()
        with scope("fullstate"):
            for m in range(M):
                full_state(m)

    @pl.when(last)
    def _():
        for load in loads[8:]:
            load.wait()

    @pl.when(jnp.logical_not(last))
    def _():
        for m in range(M):
            for k in range(NC + 1):
                f_copy(m, k).wait_send()
            for r in range(3):
                f_row(m, r).wait_send()

    with scope("BWD"):
        lax.fori_loop(0, M, backward, 0)

    @pl.when(last)
    def _():
        chunked()
        for m in range(M):
            tap_part(m)

    @pl.when(jnp.logical_not(first))
    def _():
        kp().start()
        store_grad(0, pooled_c, lift_s)
        store_grad(2, narrow_c, gnar_s)
        store_grad(1, hidden_c, total_s)

        @pl.when(last)
        def _():
            for m in range(M):
                stem_part(m)

        stem_out(1, S)
        join_pair(0)

    kp().wait_recv()
    gk_pair[...] = gk[...] + gk_got[...]
    others(Q, mine, lambda q: kx(q, mine).start())
    join_pair(2)
    join_pair(1)

    @pl.when(jnp.logical_not(first))
    def _():
        stem_out(-1, 0)

    gk_sum[...] = gk_pair[...]

    def add_kx(q):
        kx(q, q).wait_recv()
        gk_sum[...] += gk_x[q]

    others(Q, mine, add_kx)
    others(T, strip, lambda h: ky(h, strip).start())

    def out_copy(i):
        src, dst = ((h_down, o_down), (h_mix, o_mix), (h_up, o_up), (h_taps, o_taps))[i]
        return pltpu.make_async_copy(src, dst, load_s.at[i])

    def stem_copy_out(h, src):
        return pltpu.make_async_copy(src.at[h], o_stem.at[pl.ds(h * M, M)], load_s.at[4 + h])

    def gy_copy(h, sh):
        return remote(
            stem_sum.at[h], stem_far.at[sh], gy_ss.at[h], gy_rs.at[sh], {"strip": h}
        )

    def stem_total():
        def landed(k):
            g_copy(k, k).wait_recv()

        others(S, col, landed)
        for h in range(T):
            for m in range(M):
                total = gs_recv[0, m, h]
                for k in range(1, S):
                    total = total + gs_recv[k, m, h]
                stem_sum[h, m] = total
        others(T, strip, lambda h: gy_copy(h, strip).start())

    with scope("w_stem1"):
        pl.when(first)(stem_total)

    for i in (0, 2, 1):

        def add_x(q):
            x1_copy(i, q, q).wait_recv()
            accs[i][par, mine, 0] += fxs[i][q]

        with scope("w_addx"):
            others(Q, mine, add_x)
            others(T, strip, lambda h: y2_copy(i, h, strip).start())

        def add_y(h):
            y1_copy(i, h, h).wait_recv()
            for q in range(Q):
                accs[i][par, q, 1, strip] += fys[i][h, q]

        with scope("w_addy"):
            others(T, strip, add_y)
            others(Q, mine, lambda q: x2_copy(i, q, mine).start())

    @pl.when(jnp.logical_not(first))
    def _():
        with scope("w_stem2"):
            stem_out(-S, -1)
            stem_total()

    def add_ky(h):
        ky(h, h).wait_recv()

    others(T, strip, add_ky)
    share_k = gk_sum[...]
    for h in range(T):
        share_k = share_k + jnp.where(strip != h, gk_y[h], 0.0)
    w = C1 // n
    share = share_k[0:9, 0:w]
    for k in range(1, n):
        share = jnp.where(dp * T + strip == k, share_k[0:9, k * w : (k + 1) * w], share)
    h_taps[...] = share
    out_copy(3).start()

    for i, out in ((0, h_down), (2, h_up), (1, h_mix)):

        def last_y(h):
            y2_copy(i, h, h).wait_recv()
            accs[i][par, mine, 0, strip] += gys[i][h]

        with scope("w_lasty"):
            others(T, strip, last_y)

        def last_x(q):
            x2_copy(i, q, q).wait_recv()
            accs[i][par, mine, 1, strip] += gxs[i][q]

        with scope("w_lastx"):
            others(Q, mine, last_x)
        half = accs[i].shape[4]
        out[0:half] = accs[i][par, mine, 0, strip]
        out[half:] = accs[i][par, mine, 1, strip][0 : out.shape[0] - half]
        out_copy(i).start()
        if i == 0:
            for h in range(T):

                @pl.when(strip != h)
                def _():
                    gy_copy(h, h).wait_recv()
                    stem_copy_out(h, stem_far).start()

                @pl.when(strip == h)
                def _():
                    stem_copy_out(h, stem_sum).start()

    for m in range(M):
        for h in range(T):

            @pl.when(strip != h)
            def _():
                stem_copy(h, m, strip).wait_send()
                lab_copy(h, m, strip).wait_send()

                @pl.when(jnp.logical_not(last))
                def _():
                    lab_copy(h, m, h).wait_recv()

        @pl.when(jnp.logical_not(first))
        def _():
            for k in range(NC + 1):
                b_copy(m, k).wait_send()
            for r in range(3):
                b_row(m, r).wait_send()

    def sent_stem(k):
        g_copy(k, col).wait_send()

    others(S, col, sent_stem)
    others(T, strip, lambda h: gy_copy(h, strip).wait_send())
    kp().wait_send()
    others(Q, mine, lambda q: kx(q, mine).wait_send())
    others(T, strip, lambda h: ky(h, strip).wait_send())
    for i in range(3):
        p_copy(i).wait_send()

        def sent_x(q):
            x1_copy(i, q, mine).wait_send()
            x2_copy(i, q, mine).wait_send()

        def sent_y(h):
            y1_copy(i, h, strip).wait_send()
            y2_copy(i, h, strip).wait_send()

        others(Q, mine, sent_x)
        others(T, strip, sent_y)

    for i in range(4):
        out_copy(i).wait()
    for h in range(T):
        stem_copy_out(h, stem_sum).wait()


def finish(*refs):
    for source, target in zip(refs[:4], refs[5:9]):
        target[...] = source[...].reshape(target.shape)
    refs[9][...] = refs[4][...]


def shards(stem, labels, up, mix, down, taps, gain1, gain2, lat1, lat2, cls):
    B, rl, W, C1 = stem.shape
    C2 = up.shape[1]
    S, D, T = lax.axis_size("col"), lax.axis_size("dp"), lax.axis_size("strip")
    M = B // T
    RW = rl * W
    pix = T * RW
    small = pix // 4
    wc = W // S
    n = D * T
    Q = D // 2
    p1, p2 = up_to(C1 // n, 16), up_to(C2 // n, 16)
    halves = ((p1 // 2, C2), (p1 // 2, C1), (p2 // 2, C1))
    step = 384
    cuts = tuple((a, min(a + step, C2)) for a in range(0, C2, step))
    NC = len(cuts)
    npix = float(B * D * rl * T * W)
    V = pltpu.VMEM
    dma = pltpu.SemaphoreType.DMA
    vspec = pl.BlockSpec(memory_space=pltpu.VMEM)
    hspec = pl.BlockSpec(memory_space=pltpu.HBM)
    held = [
        stem.reshape(B, RW, C1), up[0], mix[0], down[0], taps[0], gain1, gain2, labels,
        lat1, lat2, cls.T,
    ]
    outs = pl.pallas_call(
        functools.partial(kernel, S, D, T, M, rl, W, npix, cuts),
        out_shape=(
            jax.ShapeDtypeStruct((C2 // n, C1), f32),
            jax.ShapeDtypeStruct((C1 // n, C1), f32),
            jax.ShapeDtypeStruct((C1 // n, C2), f32),
            jax.ShapeDtypeStruct((9, C1 // n), f32),
            jax.ShapeDtypeStruct((B, rl, wc, C1), f32),
        ),
        in_specs=[hspec] * len(held),
        out_specs=(hspec,) * 5,
        scratch_shapes=[
            V((C2 // n, C1), f32),
            V((C1 // n, C1), f32),
            V((C1 // n, C2), f32),
            V((9, C1 // n), f32),
            *[V(a.shape, a.dtype) for a in held],
            V((T, M, 4, RW // 4, C1), f32),
            V((M, 4, T, RW // 4, C1), f32),
            V((M, T, rl, W), jnp.int32),
            V((M, 3, small, C1), f32),
            V((M, NC, small, step), f32),
            V((M, 3, small, C1), f32),
            V((M, NC, small, step), f32),
            V((M, 3, small, C1), f32),
            V((M, NC, small, step), f32),
            V((M, 3, small, C1), f32),
            V((M, NC, small, step), f32),
            V((M, small, C1), f32),
            V((M, small, C1), f32),
            V((M, small, C1), f32),
            V((M, small, C1), f32),
            V((M, 3, small, C1), f32),
            V((M * pix, n * p1), bf16),
            V((M * small, n * p1), bf16),
            V((M * small, n * p2), bf16),
            V((M, pix, C1), f32),
            V((M, pix, C1), f32),
            V((M, pix, C1), f32),
            V((M, pix, C1), f32),
            V((M, pix, C1), bf16),
            V((M, small, C2), bf16),
            V((M, small, C1), bf16),
            V((M, NC, small, step), f32),
            V((M, pix, C1), bf16),
            V((M, small, C2), bf16),
            V((M, small, C1), bf16),
            V((up_to(C1, 128) // 128, T * rl, W, 128), f32),
            V((S, M, T, rl, wc, C1), f32),
            V((S, M, T, rl, wc, C1), f32),
            V((T, M, rl, wc, C1), f32),
            V((T, M, rl, wc, C1), f32),
            *[V((2, Q, 2, T, h, c), f32) for h, c in halves],
            *[V((Q, 2, T, h, c), f32) for h, c in halves],
            *[V((Q, T, h, c), f32) for h, c in halves],
            *[V((T, Q, h, c), f32) for h, c in halves],
            *[V((Q, h, c), f32) for h, c in halves],
            *[V((T, h, c), f32) for h, c in halves],
            V((16, C1), f32),
            V((16, C1), f32),
            V((16, C1), f32),
            V((Q, 16, C1), f32),
            V((16, C1), f32),
            V((T, 16, C1), f32),
            dma((max(len(held), 4 + T),)),
            dma((T, M)),
            dma((T, M)),
            dma((T, M)),
            dma((T, M)),
            dma((M, NC + 1)),
            dma((M, NC + 1)),
            dma((S,)),
            dma((S,)),
            dma((T,)),
            dma((T,)),
            dma((3,)),
            dma((3,)),
            dma((3, Q - 1)),
            dma((3, Q - 1)),
            dma((3, T - 1)),
            dma((3, T - 1)),
            dma((3, Q - 1)),
            dma((3, Q - 1)),
            dma((3, T - 1)),
            dma((3, T - 1)),
            dma((3, max(Q, T))),
            dma((3, max(Q, T))),
            dma((M, 3)),
            dma((M, 3)),
        ],
        compiler_params=pltpu.CompilerParams(
            collective_id=0, has_side_effects=True, vmem_limit_bytes=60000 * 1024
        ),
        name="columns",
    )(*held)
    tall = lambda a: jax.ShapeDtypeStruct((a.shape[0], 1, a.shape[1]), f32)
    done = pl.pallas_call(
        finish,
        out_shape=tuple(tall(a) for a in outs[:4])
        + (jax.ShapeDtypeStruct(outs[4].shape, f32),),
        in_specs=[vspec] * 5,
        out_specs=(vspec,) * 5,
        name="finish",
    )(*outs)
    return tuple(jnp.transpose(a, (1, 0, 2)) for a in done[:4]) + (done[4],)


def solution(mesh):
    placed = (
        P("dp", "strip", None, None),
        P("dp", "strip", None),
        P("col", None, None),
        P("col", None, None),
        P("col", None, None),
        P("col", None, None),
        P("col", None),
        P("col", None),
        P(),
        P(),
        P(),
    )
    return jax.shard_map(
        shards,
        mesh=mesh,
        in_specs=placed,
        out_specs=(
            P("col", ("dp", "strip"), None),
            P("col", ("dp", "strip"), None),
            P("col", ("dp", "strip"), None),
            P("col", None, ("dp", "strip")),
            P("dp", "strip", "col", None),
        ),
        check_vma=False,
    )
```

```python
import contextlib
import functools

import jax
import jax.numpy as jnp
from jax import lax
from jax.experimental import pallas as pl
from jax.experimental.pallas import tpu as pltpu
from jax.sharding import PartitionSpec as P

loss_scale = 64.0
root_coef = 0.7978845608028654
cube_coef = 0.044715
f32 = jnp.float32
bf16 = jnp.bfloat16
MESH = pl.DeviceIdType.MESH
scope = contextlib.nullcontext


def gelu_pair(values):
    square = values * values
    tangent = jnp.tanh(root_coef * (values + cube_coef * values * square))
    half = 0.5 * (1.0 + tangent)
    slope = half + 0.5 * values * (1.0 - tangent * tangent) * root_coef * (
        1.0 + 3.0 * cube_coef * square
    )
    return values * half, slope


def dot(left, right):
    return jnp.dot(left, right, preferred_element_type=f32)


def dot_back(left, right):
    return lax.dot_general(left, right, (((1,), (1,)), ((), ())), preferred_element_type=f32)


def dot_outer(left, right):
    return lax.dot_general(left, right, (((0,), (0,)), ((), ())), preferred_element_type=f32)


def up_to(count, multiple):
    return -(-count // multiple) * multiple


def spread(count, owners, T):
    parts = owners * T
    run = count // parts
    half = up_to(run, 16) // 2
    source = lax.broadcasted_iota(jnp.int32, (count, 1), 0)
    target = source
    before = 0
    for owner in range(owners):
        for h in range(T):
            for side in range(2):
                begin = (owner * T + h) * run + side * half
                place = (owner % 2) * (owners // 2) + owner // 2
                shift = ((place * 2 + side) * T + h) * half - begin
                target = target + jnp.where(source >= begin, shift - before, 0)
                before = shift
    spot = lax.broadcasted_iota(jnp.int32, (count, parts * 2 * half), 1)
    return (spot == target).astype(f32).astype(bf16)


def phase_matrix(rl, W):
    count, wide, quarter = rl * W, W // 2, rl * W // 4
    out = lax.broadcasted_iota(jnp.int32, (count, count), 0)
    source = lax.broadcasted_iota(jnp.int32, (count, count), 1)
    hit = jnp.zeros((count, count), jnp.bool_)
    for ri in range(2):
        for ci in range(2):
            for row in range(rl // 2):
                rest = out - ((2 * ri + ci) * quarter + row * wide)
                inside = (rest >= 0) & (rest < wide)
                hit = hit | (inside & (source == (2 * row + ri) * W + ci + 2 * rest))
    return hit.astype(f32).astype(bf16)


def kernel(
    S, D, T, M, rl, W, npix, cuts,
    stem_h, up_h, mix_h, down_h, taps_h, gain1_h, gain2_h, labels_h, lat1_h, lat2_h, cls_h,
    o_up, o_mix, o_down, o_taps, o_stem,
    h_up, h_mix, h_down, h_taps,
    stem, up, mix, down, taps, gain1, gain2, labels, lat1, lat2, cls,
    stem_send, stem_full, lab_full, in1, in2, out1, out2, cin1, cin2, cout1, cout2,
    inp, outp, cinp, coutp, branch_s, hidden_c, pooled_c, narrow_c,
    grad_depth_s, grad_mixture_s, mixture_s, slope1_s, hidden_s, narrow_s, pooled_s, slope2_s, total_s, lift_s, gnar_s,
    natural, gs_send, gs_recv, stem_sum, stem_far,
    acc_d, acc_m, acc_u, got_d, got_m, got_u, fx_d, fx_m, fx_u, fy_d, fy_m, fy_u,
    gx_d, gx_m, gx_u, gy_d, gy_m, gy_u, gk, gk_got, gk_pair, gk_x, gk_sum, gk_y,
    load_s, pair_s,
    stem_ss, stem_rs, lab_ss, lab_rs, f_ss, f_rs, g_ss, g_rs, gy_ss, gy_rs,
    p_ss, p_rs, x1_ss, x1_rs, y1_ss, y1_rs, x2_ss, x2_rs, y2_ss, y2_rs,
    k_ss, k_rs, ff_ss, ff_rs,
):
    col, dp, strip = lax.axis_index("col"), lax.axis_index("dp"), lax.axis_index("strip")
    first, last = col == 0, col == S - 1
    C1, C2 = up.shape[1], up.shape[0]
    pix = T * rl * W
    small = pix // 4
    rows = T * rl
    wide = W // 2
    wc = W // S
    NC = len(cuts)
    lanes = [(a, min(a + 128, C1)) for a in range(0, C1, 128)]
    par = lax.rem(dp, 2)
    mine = dp // 2
    Q = D // 2

    def remote(src, dst, ss, rs, target):
        return pltpu.make_async_remote_copy(
            src_ref=src, dst_ref=dst, send_sem=ss, recv_sem=rs,
            device_id=target, device_id_type=MESH,
        )

    gate = pltpu.get_barrier_semaphore()
    for h in range(T):
        for k in range(S):

            @pl.when((col != k) | (strip != h))
            def _():
                pl.semaphore_signal(
                    gate, inc=1, device_id={"col": k, "strip": h}, device_id_type=MESH
                )

        for d in range(D):

            @pl.when(dp != d)
            def _():
                pl.semaphore_signal(
                    gate, inc=1, device_id={"dp": d, "strip": h}, device_id_type=MESH
                )

    loads = [
        pltpu.make_async_copy(src, dst, load_s.at[i])
        for i, (src, dst) in enumerate(
            ((stem_h, stem), (up_h, up), (mix_h, mix), (down_h, down),
             (taps_h, taps), (gain1_h, gain1), (gain2_h, gain2), (labels_h, labels),
             (lat1_h, lat1), (lat2_h, lat2), (cls_h, cls))
        )
    ]
    for load in loads[:8]:
        load.start()

    @pl.when(last)
    def _():
        for load in loads[8:]:
            load.start()

    @pl.when(first)
    def _():
        in2[...] = jnp.zeros_like(in2)
        in1[...] = jnp.zeros_like(in1)
        inp[...] = jnp.zeros_like(inp)

    gk[...] = jnp.zeros_like(gk)
    order = phase_matrix(rl, W)
    loads[0].wait()
    for m in range(M):
        for h in range(T):
            stem_send[h, m] = dot(order, stem[h * M + m]).reshape(stem_send.shape[2:])
    for load in loads[1:8]:
        load.wait()
    with scope("gatewait"):
        pl.semaphore_wait(gate, S * T - 1 + (D - 1) * T)

    def stem_copy(h, m, slot):
        return remote(
            stem_send.at[h, m], stem_full.at[m, :, slot], stem_ss.at[h, m], stem_rs.at[slot, m],
            {"strip": h},
        )

    def lab_copy(h, m, slot):
        return remote(
            labels.at[h * M + m], lab_full.at[m, slot], lab_ss.at[h, m], lab_rs.at[slot, m],
            {"strip": h},
        )

    pair = {"dp": dp + 1 - 2 * par}

    @pl.when(par == 0)
    def _():
        pl.semaphore_wait(pair_s, 1)

    for m in range(M):
        for h in range(T):

            @pl.when(strip != h)
            def _():
                stem_copy(h, m, strip).start()

    @pl.when(par == 1)
    def _():
        for m in range(M):
            for h in range(T):

                @pl.when(strip != h)
                def _():
                    stem_copy(h, m, strip).wait_send()

        pl.semaphore_signal(pair_s, inc=1, device_id=pair, device_id_type=MESH)

    for m in range(M):
        for h in range(T):

            @pl.when(strip != h)
            def _():
                lab_copy(h, m, strip).start()

            @pl.when(strip == h)
            def _():
                stem_full[m, :, h] = stem_send[h, m]
                lab_full[m, h] = labels[h * M + m]

    kern = taps[0:9].astype(f32)
    g1 = gain1[...]
    g2 = gain2[...]
    place = lax.rem(lax.broadcasted_iota(jnp.int32, (small, 1), 0), wide)
    not_low = place != 0
    not_high = place != wide - 1

    def split(values):
        return [[values[(2 * ri + ci) * small :][:small] for ci in range(2)] for ri in range(2)]

    def join(parts):
        return jnp.concatenate([parts[ri][ci] for ri in range(2) for ci in range(2)], axis=0)

    def pool(values):
        return (values[0:small] + values[small : 2 * small]) + (
            values[2 * small : 3 * small] + values[3 * small :]
        )

    def sources(parts):
        found = []
        for ri in range(2):
            even, odd = parts[ri]
            before = jnp.where(not_low, pltpu.roll(odd, 1, 0), 0.0)
            after = jnp.where(not_high, pltpu.roll(even, small - 1, 0), 0.0)
            found.append(((before, even, odd), (even, odd, after)))
        return found

    def rows_moved(values, step):
        if step == 0:
            return values
        blank = jnp.zeros((wide, values.shape[1]), f32)
        if step > 0:
            return jnp.concatenate([values[wide:], blank], axis=0)
        return jnp.concatenate([blank, values[:-wide]], axis=0)

    def depthwise(values, sign):
        found = sources(split(values))
        parts = [[None, None], [None, None]]
        for ri in range(2):
            for ci in range(2):
                total = None
                for i in (-1, 0, 1):
                    line = None
                    for j in (-1, 0, 1):
                        t = 3 * (sign * i + 1) + (sign * j + 1)
                        term = kern[t : t + 1] * found[(ri + i) % 2][ci][j + 1]
                        line = term if line is None else line + term
                    line = rows_moved(line, (ri + i) // 2)
                    total = line if total is None else total + line
                parts[ri][ci] = total
        return join(parts)

    def tap_sums(values, grads):
        found, grads = sources(split(values)), split(grads)
        lines = []
        for i in (-1, 0, 1):
            for j in (-1, 0, 1):
                total = None
                for ri in range(2):
                    for ci in range(2):
                        window, grad = found[(ri + i) % 2][ci][j + 1], grads[ri][ci]
                        step = (ri + i) // 2
                        if step > 0:
                            window, grad = window[wide:], grad[:-wide]
                        elif step < 0:
                            window, grad = window[:-wide], grad[wide:]
                        both = window * grad
                        for at in range(0, both.shape[0], wide):
                            piece = both[at : at + wide]
                            total = piece if total is None else total + piece
                lines.append(jnp.sum(total, axis=0, keepdims=True))
        return lines

    def f_copy(m, k):
        src, dst = (out2.at[m, k], in2.at[m, k]) if k < NC else (outp.at[m], inp.at[m])
        return remote(src, dst, f_ss.at[m, k], f_rs.at[m, k], {"col": col + 1})

    def b_copy(m, k):
        src, dst = (cout2.at[m, k], cin2.at[m, k]) if k < NC else (coutp.at[m], cinp.at[m])
        return remote(src, dst, f_ss.at[m, k], f_rs.at[m, k], {"col": col - 1})

    def f_row(m, r):
        return remote(
            out1.at[m, r], in1.at[m, r], ff_ss.at[m, r], ff_rs.at[m, r], {"col": col + 1}
        )

    def b_row(m, r):
        return remote(
            cout1.at[m, r], cin1.at[m, r], ff_ss.at[m, r], ff_rs.at[m, r], {"col": col - 1}
        )

    def forward(m, carry):
        with scope("f_stemwait"):
            for h in range(T):

                @pl.when(strip != h)
                def _():
                    stem_copy(h, m, h).wait_recv()

        risen = None
        for k, (a, b) in enumerate(cuts):
            with scope("f_wait1"):

                @pl.when(jnp.logical_not(first))
                def _():
                    f_copy(m, k).wait_recv()

            narrow = in2[m, k, :, 0 : b - a].astype(bf16)
            narrow_s[m, :, a:b] = narrow
            part = dot(narrow, up[a:b])
            risen = part if risen is None else risen + part
        mixture = stem_full[m].reshape(pix, C1) + jnp.concatenate([risen] * 4, axis=0)
        mixture_s[m] = mixture
        active, slope = gelu_pair(depthwise(mixture, 1))
        slope1_s[m] = slope
        hidden = active.astype(bf16)
        hidden_s[m] = hidden
        branch = dot(hidden, mix[...])
        branch_s[m] = branch[small:].reshape(branch_s.shape[1:])
        pool_branch = pool(branch)

        with scope("f_wait2"):

            @pl.when(jnp.logical_not(first))
            def _():
                f_copy(m, NC).wait_recv()

        low1 = g1 * inp[m] + pool_branch
        outp[m] = low1
        pooled = (low1 * 0.25).astype(bf16)
        pooled_s[m] = pooled
        grown = [dot(pooled, down[:, a:b]) for a, b in cuts]
        for k, (a, b) in enumerate(cuts):
            lifted, slope2 = gelu_pair(grown[k])
            slope2_s[m, k, :, 0 : b - a] = slope2
            out2[m, k, :, 0 : b - a] = g2[:, a:b] * in2[m, k, :, 0 : b - a] + lifted

            @pl.when(jnp.logical_not(last))
            def _():
                f_copy(m, k).start()

        @pl.when(jnp.logical_not(last))
        def _():
            f_copy(m, NC).start()

        return carry

    with scope("FWD"):
        lax.fori_loop(0, M, forward, 0)

    def full_state(m):
        for r in range(3):

            @pl.when(jnp.logical_not(first))
            def _():
                f_row(m, r).wait_recv()

            out1[m, r] = g1 * in1[m, r] + branch_s[m, r]

            @pl.when(jnp.logical_not(last))
            def _():
                f_row(m, r).start()

    def g_copy(k, sk):
        return remote(gs_send.at[k], gs_recv.at[sk], g_ss.at[k], g_rs.at[sk], {"col": k})

    def stem_out(low, high):
        for k in range(S):

            @pl.when((col != k) & (k >= col + low) & (k < col + high))
            def _():
                g_copy(k, col).start()

    n = D * T
    flat = lambda ref: ref[...].reshape(-1, ref.shape[-1])
    accs, gots = (acc_d, acc_m, acc_u), (got_d, got_m, got_u)
    fxs, fys = (fx_d, fx_m, fx_u), (fy_d, fy_m, fy_u)
    gxs, gys = (gx_d, gx_m, gx_u), (gy_d, gy_m, gy_u)

    def chunked():
        pick = spread(C1, D, T)
        hidden_c[...] = dot(flat(hidden_s), pick).astype(bf16)
        pooled_c[...] = dot(flat(pooled_s), pick).astype(bf16)
        narrow_c[...] = dot(flat(narrow_s), spread(C2, D, T)).astype(bf16)

    partner = {"dp": dp + 1 - 2 * par}

    def rel(a, b, count):
        return 0 if count == 2 else lax.rem(a - b - 1 + count, count)

    def ends(other, source, me, count):
        back = rel(me, other, count) if source is me else rel(other, me, count)
        return rel(other, me, count), back

    def p_copy(i):
        return remote(accs[i].at[1 - par], gots[i], p_ss.at[i], p_rs.at[i], partner)

    def x1_copy(i, q, sq):
        a, b = ends(q, sq, mine, Q)
        return remote(
            accs[i].at[par, q, 0], fxs[i].at[sq], x1_ss.at[i, a], x1_rs.at[i, b],
            {"dp": 2 * q + par},
        )

    def y1_copy(i, h, sh):
        a, b = ends(h, sh, strip, T)
        return remote(
            accs[i].at[par, :, 1, h], fys[i].at[sh], y1_ss.at[i, a], y1_rs.at[i, b],
            {"strip": h},
        )

    def x2_copy(i, q, sq):
        a, b = ends(q, sq, mine, Q)
        return remote(
            accs[i].at[par, q, 1, strip], gxs[i].at[sq], x2_ss.at[i, a], x2_rs.at[i, b],
            {"dp": 2 * q + par},
        )

    def y2_copy(i, h, sh):
        a, b = ends(h, sh, strip, T)
        return remote(
            accs[i].at[par, mine, 0, h], gys[i].at[sh], y2_ss.at[i, a], y2_rs.at[i, b],
            {"strip": h},
        )

    def store_grad(i, left, right):
        accs[i][...] = dot_outer(left[...], flat(right)).reshape(accs[i].shape)
        p_copy(i).start()

    def others(count, me, act):
        for t in range(count):

            @pl.when(me != t)
            def _():
                act(t)

    def join_pair(i):
        with scope("w_pair"):
            p_copy(i).wait_recv()
            accs[i][par] += gots[i][...]
            others(Q, mine, lambda q: x1_copy(i, q, mine).start())

        others(T, strip, lambda h: y1_copy(i, h, strip).start())

    def head(m):
        with scope("h_state"):
            full_state(m)
            for h in range(T):

                @pl.when(strip != h)
                def _():
                    lab_copy(h, m, h).wait_recv()

        rest = [out1[m, r] for r in range(3)]
        state = jnp.concatenate([outp[m] - (rest[0] + rest[1] + rest[2])] + rest, axis=0)
        wide2 = None
        for k, (a, b) in enumerate(cuts):
            part = dot(out2[m, k, :, 0 : b - a].astype(bf16), lat2[a:b])
            wide2 = part if wide2 is None else wide2 + part
        lateral = dot(state.astype(bf16), lat1[...])
        lateral = jnp.concatenate(
            [lateral[at : at + small] + wide2 for at in range(0, pix, small)], axis=0
        )
        active, slope = gelu_pair(lateral)
        logits = dot_back(active.astype(bf16), cls[...])
        shifted = jnp.exp(logits - jnp.max(logits, axis=-1, keepdims=True))
        probs = shifted / jnp.sum(shifted, axis=-1, keepdims=True)
        lane = lax.broadcasted_iota(jnp.int32, (wide, W), 1)
        line = lax.broadcasted_iota(jnp.int32, (wide, W), 0)
        found = []
        for ri in range(2):
            for ci in range(2):
                for h in range(T):
                    block = lab_full[m, h].astype(f32)
                    for row in range(rl // 2):
                        r = 2 * row + ri
                        turned = jnp.where(lane == 2 * line + ci, block[r : r + 1], 0.0)
                        found.append(jnp.sum(turned, axis=1, keepdims=True))
        label = jnp.concatenate(found, axis=0).astype(jnp.int32)
        onehot = (lax.broadcasted_iota(jnp.int32, logits.shape, 1) == label).astype(f32)
        grad_logits = (probs - onehot) * (loss_scale / npix)
        grad_lat = dot(grad_logits.astype(bf16), cls[...]) * slope
        cot1 = dot_back(grad_lat.astype(bf16), lat1[...])
        cinp[m] = cot1[0:small]
        for r in range(3):
            cin1[m, r] = cot1[(r + 1) * small :][:small] - cot1[0:small]
        pooled_lat = pool(grad_lat).astype(bf16)
        for k, (a, b) in enumerate(cuts):
            cin2[m, k, :, 0 : b - a] = dot_back(pooled_lat, lat2[a:b])

    def k_copy(stage, src, dst, target, t, st):
        return remote(src, dst, k_ss.at[stage, t], k_rs.at[stage, st], target)

    def kp():
        return k_copy(0, gk, gk_got, partner, 0, 0)

    def kx(q, sq):
        return k_copy(1, gk_pair, gk_x.at[sq], {"dp": 2 * q + par}, q, sq)

    def ky(h, sh):
        return k_copy(2, gk_sum, gk_y.at[sh], {"strip": h}, h, sh)

    def tap_part(m):
        for t, line in enumerate(tap_sums(mixture_s[m], grad_depth_s[m])):
            gk[t : t + 1] += line

    def stem_part(m):
        parts = split(grad_mixture_s[m])
        for ri in range(2):
            for ci in range(2):
                for row in range(rows // 2):
                    for at, (a, b) in enumerate(lanes):
                        natural[at, 2 * row + ri, pl.ds(ci, wide, stride=2), 0 : b - a] = parts[
                            ri
                        ][ci][row * wide : (row + 1) * wide, a:b]
        for k in range(S):
            for h in range(T):
                for at, (a, b) in enumerate(lanes):
                    gs_send[k, m, h, :, :, a:b] = natural[
                        at, h * rl : (h + 1) * rl, k * wc : (k + 1) * wc, 0 : b - a
                    ]
        for k in range(S):

            @pl.when(col == k)
            def _():
                gs_recv[k, m] = gs_send[k, m]

        @pl.when(first & (m == M - 1))
        def _():
            stem_out(1, S)

    def backward(m, carry):
        final = first & (m == M - 1)

        @pl.when(last)
        def _():
            with scope("HEAD"):
                head(m)

        with scope("b_rows"):
            for r in range(3):

                @pl.when(jnp.logical_not(last))
                def _():
                    b_row(m, r).wait_recv()

                @pl.when(jnp.logical_not(first))
                def _():
                    cout1[m, r] = g1 * cin1[m, r]
                    b_row(m, r).start()

        risen = None
        for k, (a, b) in enumerate(cuts):
            with scope("b_wait1"):

                @pl.when(jnp.logical_not(last))
                def _():
                    b_copy(m, k).wait_recv()

            lift = (cin2[m, k, :, 0 : b - a] * slope2_s[m, k, :, 0 : b - a]).astype(bf16)
            lift_s[m, :, a:b] = lift
            part = dot_back(lift, down[:, a:b])
            risen = part if risen is None else risen + part

        with scope("b_wait2"):

            @pl.when(jnp.logical_not(last))
            def _():
                b_copy(m, NC).wait_recv()

        low = cinp[m] + risen * 0.25

        @pl.when(jnp.logical_not(first))
        def _():
            coutp[m] = g1 * low
            b_copy(m, NC).start()

        total = jnp.concatenate([low] + [low + cin1[m, r] for r in range(3)], axis=0)
        total_narrow = total.astype(bf16)
        total_s[m] = total_narrow

        @pl.when(final)
        def _():
            store_grad(0, pooled_c, lift_s)

        grad_depth = dot_back(total_narrow, mix[...]) * slope1_s[m]
        grad_mixture = depthwise(grad_depth, -1)
        grad_narrow = pool(grad_mixture).astype(bf16)
        gnar_s[m] = grad_narrow

        @pl.when(jnp.logical_not(first))
        def _():
            for k, (a, b) in enumerate(cuts):
                cout2[m, k, :, 0 : b - a] = g2[:, a:b] * cin2[m, k, :, 0 : b - a] + dot_back(
                    grad_narrow, up[a:b]
                )
                with scope("b_send1"):
                    b_copy(m, k).start()

        grad_depth_s[m] = grad_depth
        grad_mixture_s[m] = grad_mixture

        @pl.when(final)
        def _():
            store_grad(2, narrow_c, gnar_s)
            store_grad(1, hidden_c, total_s)

        @pl.when(jnp.logical_not(last))
        def _():
            tap_part(m)

            @pl.when(final)
            def _():
                kp().start()
                join_pair(0)

            stem_part(m)

        return carry

    @pl.when(jnp.logical_not(last))
    def _():
        chunked()
        with scope("fullstate"):
            for m in range(M):
                full_state(m)

    @pl.when(last)
    def _():
        for load in loads[8:]:
            load.wait()

    @pl.when(jnp.logical_not(last))
    def _():
        for m in range(M):
            for k in range(NC + 1):
                f_copy(m, k).wait_send()
            for r in range(3):
                f_row(m, r).wait_send()

    with scope("BWD"):
        lax.fori_loop(0, M, backward, 0)

    @pl.when(last)
    def _():
        chunked()
        for m in range(M):
            tap_part(m)

    @pl.when(jnp.logical_not(first))
    def _():
        kp().start()
        store_grad(0, pooled_c, lift_s)
        store_grad(2, narrow_c, gnar_s)
        store_grad(1, hidden_c, total_s)

        @pl.when(last)
        def _():
            for m in range(M):
                stem_part(m)

        stem_out(1, S)
        join_pair(0)

    kp().wait_recv()
    gk_pair[...] = gk[...] + gk_got[...]
    others(Q, mine, lambda q: kx(q, mine).start())
    join_pair(2)
    join_pair(1)

    @pl.when(jnp.logical_not(first))
    def _():
        stem_out(-1, 0)

    gk_sum[...] = gk_pair[...]

    def add_kx(q):
        kx(q, q).wait_recv()
        gk_sum[...] += gk_x[q]

    others(Q, mine, add_kx)
    others(T, strip, lambda h: ky(h, strip).start())

    def out_copy(i):
        src, dst = ((h_down, o_down), (h_mix, o_mix), (h_up, o_up), (h_taps, o_taps))[i]
        return pltpu.make_async_copy(src, dst, load_s.at[i])

    def stem_copy_out(h, src):
        return pltpu.make_async_copy(src.at[h], o_stem.at[pl.ds(h * M, M)], load_s.at[4 + h])

    def gy_copy(h, sh):
        return remote(
            stem_sum.at[h], stem_far.at[sh], gy_ss.at[h], gy_rs.at[sh], {"strip": h}
        )

    def stem_total():
        def landed(k):
            g_copy(k, k).wait_recv()

        others(S, col, landed)
        for h in range(T):
            for m in range(M):
                total = gs_recv[0, m, h]
                for k in range(1, S):
                    total = total + gs_recv[k, m, h]
                stem_sum[h, m] = total
        others(T, strip, lambda h: gy_copy(h, strip).start())

    with scope("w_stem1"):
        pl.when(first)(stem_total)

    for i in (0, 2, 1):

        def add_x(q):
            x1_copy(i, q, q).wait_recv()
            accs[i][par, mine, 0] += fxs[i][q]

        with scope("w_addx"):
            others(Q, mine, add_x)
            others(T, strip, lambda h: y2_copy(i, h, strip).start())

        def add_y(h):
            y1_copy(i, h, h).wait_recv()
            for q in range(Q):
                accs[i][par, q, 1, strip] += fys[i][h, q]

        with scope("w_addy"):
            others(T, strip, add_y)
            others(Q, mine, lambda q: x2_copy(i, q, mine).start())

    @pl.when(jnp.logical_not(first))
    def _():
        with scope("w_stem2"):
            stem_out(-S, -1)
            stem_total()

    def add_ky(h):
        ky(h, h).wait_recv()

    others(T, strip, add_ky)
    share_k = gk_sum[...]
    for h in range(T):
        share_k = share_k + jnp.where(strip != h, gk_y[h], 0.0)
    w = C1 // n
    share = share_k[0:9, 0:w]
    for k in range(1, n):
        share = jnp.where(dp * T + strip == k, share_k[0:9, k * w : (k + 1) * w], share)
    h_taps[...] = share
    out_copy(3).start()

    for i, out in ((0, h_down), (2, h_up), (1, h_mix)):

        def last_y(h):
            y2_copy(i, h, h).wait_recv()
            accs[i][par, mine, 0, strip] += gys[i][h]

        with scope("w_lasty"):
            others(T, strip, last_y)

        def last_x(q):
            x2_copy(i, q, q).wait_recv()
            accs[i][par, mine, 1, strip] += gxs[i][q]

        with scope("w_lastx"):
            others(Q, mine, last_x)
        half = accs[i].shape[4]
        out[0:half] = accs[i][par, mine, 0, strip]
        out[half:] = accs[i][par, mine, 1, strip][0 : out.shape[0] - half]
        out_copy(i).start()
        if i == 0:
            for h in range(T):

                @pl.when(strip != h)
                def _():
                    gy_copy(h, h).wait_recv()
                    stem_copy_out(h, stem_far).start()

                @pl.when(strip == h)
                def _():
                    stem_copy_out(h, stem_sum).start()

    for m in range(M):
        for h in range(T):

            @pl.when(strip != h)
            def _():
                pl.when(par == 0)(lambda: stem_copy(h, m, strip).wait_send())
                lab_copy(h, m, strip).wait_send()

                @pl.when(jnp.logical_not(last))
                def _():
                    lab_copy(h, m, h).wait_recv()

        @pl.when(jnp.logical_not(first))
        def _():
            for k in range(NC + 1):
                b_copy(m, k).wait_send()
            for r in range(3):
                b_row(m, r).wait_send()

    def sent_stem(k):
        g_copy(k, col).wait_send()

    others(S, col, sent_stem)
    others(T, strip, lambda h: gy_copy(h, strip).wait_send())
    kp().wait_send()
    others(Q, mine, lambda q: kx(q, mine).wait_send())
    others(T, strip, lambda h: ky(h, strip).wait_send())
    for i in range(3):
        p_copy(i).wait_send()

        def sent_x(q):
            x1_copy(i, q, mine).wait_send()
            x2_copy(i, q, mine).wait_send()

        def sent_y(h):
            y1_copy(i, h, strip).wait_send()
            y2_copy(i, h, strip).wait_send()

        others(Q, mine, sent_x)
        others(T, strip, sent_y)

    for i in range(4):
        out_copy(i).wait()
    for h in range(T):
        stem_copy_out(h, stem_sum).wait()


def finish(*refs):
    for source, target in zip(refs[:4], refs[5:9]):
        target[...] = source[...].reshape(target.shape)
    refs[9][...] = refs[4][...]


def shards(stem, labels, up, mix, down, taps, gain1, gain2, lat1, lat2, cls):
    B, rl, W, C1 = stem.shape
    C2 = up.shape[1]
    S, D, T = lax.axis_size("col"), lax.axis_size("dp"), lax.axis_size("strip")
    M = B // T
    RW = rl * W
    pix = T * RW
    small = pix // 4
    wc = W // S
    n = D * T
    Q = D // 2
    p1, p2 = up_to(C1 // n, 16), up_to(C2 // n, 16)
    halves = ((p1 // 2, C2), (p1 // 2, C1), (p2 // 2, C1))
    step = 384
    cuts = tuple((a, min(a + step, C2)) for a in range(0, C2, step))
    NC = len(cuts)
    npix = float(B * D * rl * T * W)
    V = pltpu.VMEM
    dma = pltpu.SemaphoreType.DMA
    vspec = pl.BlockSpec(memory_space=pltpu.VMEM)
    hspec = pl.BlockSpec(memory_space=pltpu.HBM)
    held = [
        stem.reshape(B, RW, C1), up[0], mix[0], down[0], taps[0], gain1, gain2, labels,
        lat1, lat2, cls.T,
    ]
    outs = pl.pallas_call(
        functools.partial(kernel, S, D, T, M, rl, W, npix, cuts),
        out_shape=(
            jax.ShapeDtypeStruct((C2 // n, C1), f32),
            jax.ShapeDtypeStruct((C1 // n, C1), f32),
            jax.ShapeDtypeStruct((C1 // n, C2), f32),
            jax.ShapeDtypeStruct((9, C1 // n), f32),
            jax.ShapeDtypeStruct((B, rl, wc, C1), f32),
        ),
        in_specs=[hspec] * len(held),
        out_specs=(hspec,) * 5,
        scratch_shapes=[
            V((C2 // n, C1), f32),
            V((C1 // n, C1), f32),
            V((C1 // n, C2), f32),
            V((9, C1 // n), f32),
            *[V(a.shape, a.dtype) for a in held],
            V((T, M, 4, RW // 4, C1), f32),
            V((M, 4, T, RW // 4, C1), f32),
            V((M, T, rl, W), jnp.int32),
            V((M, 3, small, C1), f32),
            V((M, NC, small, step), f32),
            V((M, 3, small, C1), f32),
            V((M, NC, small, step), f32),
            V((M, 3, small, C1), f32),
            V((M, NC, small, step), f32),
            V((M, 3, small, C1), f32),
            V((M, NC, small, step), f32),
            V((M, small, C1), f32),
            V((M, small, C1), f32),
            V((M, small, C1), f32),
            V((M, small, C1), f32),
            V((M, 3, small, C1), f32),
            V((M * pix, n * p1), bf16),
            V((M * small, n * p1), bf16),
            V((M * small, n * p2), bf16),
            V((M, pix, C1), f32),
            V((M, pix, C1), f32),
            V((M, pix, C1), f32),
            V((M, pix, C1), f32),
            V((M, pix, C1), bf16),
            V((M, small, C2), bf16),
            V((M, small, C1), bf16),
            V((M, NC, small, step), f32),
            V((M, pix, C1), bf16),
            V((M, small, C2), bf16),
            V((M, small, C1), bf16),
            V((up_to(C1, 128) // 128, T * rl, W, 128), f32),
            V((S, M, T, rl, wc, C1), f32),
            V((S, M, T, rl, wc, C1), f32),
            V((T, M, rl, wc, C1), f32),
            V((T, M, rl, wc, C1), f32),
            *[V((2, Q, 2, T, h, c), f32) for h, c in halves],
            *[V((Q, 2, T, h, c), f32) for h, c in halves],
            *[V((Q, T, h, c), f32) for h, c in halves],
            *[V((T, Q, h, c), f32) for h, c in halves],
            *[V((Q, h, c), f32) for h, c in halves],
            *[V((T, h, c), f32) for h, c in halves],
            V((16, C1), f32),
            V((16, C1), f32),
            V((16, C1), f32),
            V((Q, 16, C1), f32),
            V((16, C1), f32),
            V((T, 16, C1), f32),
            dma((max(len(held), 4 + T),)),
            pltpu.SemaphoreType.REGULAR,
            dma((T, M)),
            dma((T, M)),
            dma((T, M)),
            dma((T, M)),
            dma((M, NC + 1)),
            dma((M, NC + 1)),
            dma((S,)),
            dma((S,)),
            dma((T,)),
            dma((T,)),
            dma((3,)),
            dma((3,)),
            dma((3, Q - 1)),
            dma((3, Q - 1)),
            dma((3, T - 1)),
            dma((3, T - 1)),
            dma((3, Q - 1)),
            dma((3, Q - 1)),
            dma((3, T - 1)),
            dma((3, T - 1)),
            dma((3, max(Q, T))),
            dma((3, max(Q, T))),
            dma((M, 3)),
            dma((M, 3)),
        ],
        compiler_params=pltpu.CompilerParams(
            collective_id=0, has_side_effects=True, vmem_limit_bytes=60000 * 1024
        ),
        name="columns",
    )(*held)
    tall = lambda a: jax.ShapeDtypeStruct((a.shape[0], 1, a.shape[1]), f32)
    done = pl.pallas_call(
        finish,
        out_shape=tuple(tall(a) for a in outs[:4])
        + (jax.ShapeDtypeStruct(outs[4].shape, f32),),
        in_specs=[vspec] * 5,
        out_specs=(vspec,) * 5,
        name="finish",
    )(*outs)
    return tuple(jnp.transpose(a, (1, 0, 2)) for a in done[:4]) + (done[4],)


def solution(mesh):
    placed = (
        P("dp", "strip", None, None),
        P("dp", "strip", None),
        P("col", None, None),
        P("col", None, None),
        P("col", None, None),
        P("col", None, None),
        P("col", None),
        P("col", None),
        P(),
        P(),
        P(),
    )
    return jax.shard_map(
        shards,
        mesh=mesh,
        in_specs=placed,
        out_specs=(
            P("col", ("dp", "strip"), None),
            P("col", ("dp", "strip"), None),
            P("col", ("dp", "strip"), None),
            P("col", None, ("dp", "strip")),
            P("dp", "strip", "col", None),
        ),
        check_vma=False,
    )
```
